256 devices in a mesh: ta: 32 (over z, y_lo, core), ka: 8 (over y_hi, x).
Axes of the slice: x: 4, y: 4 (y_hi: 2, y_lo: 2; y = y_hi * 2 + y_lo), z: 8, core: 2. Of those that a mesh axis runs over, the one named last changes fastest.
Arguments:
- green_row: float32 [2, 4, 4, 64, 1024], P(None, None, None, 'ta', 'ka'), may hold values from -6 to 6
- screen_lesser: float32 [2, 4, 4, 64, 1024], P(None, None, None, 'ta', 'ka'), may hold values from -6 to 6
- screen_retarded: float32 [2, 4, 4, 64, 1024], P(None, None, None, 'ta', 'ka'), may hold values from -6 to 6
- onsite: float32 [2, 4, 4], replicated, may hold values from -3 to 3
- lesser_slab: bfloat16 [2, 4, 4, 64, 64, 1024], P(None, None, None, 'ta', None, 'ka'), may hold values from -0.5 to 0.5
- advanced_slab: bfloat16 [2, 4, 4, 64, 64, 1024], P(None, None, None, 'ta', None, 'ka'), may hold values from -0.5 to 0.5
- slab_start: int32 [1], replicated, may hold values from 0 to 4095
- block_table: int32 [32], replicated, may hold values from 0 to 31, each once
Outputs:
- next_row: float32 [2, 4, 4, 64, 1024], P(None, None, None, 'ta', 'ka')
- derivative: float32 [2, 4, 4, 64, 1024], P(None, None, None, 'ta', 'ka')
The draws below stay inside these ranges and needn't reach their ends.
Inputs may be any that keep to these rules, and one draw needn't show every extreme that they name: block_table is a permutation: each time block 0 to 31 appears once.
All inputs are finite; a program needn't handle non-finite values.
Results may differ from the reference program's by a relative error of at most 0.0019.
Values sent between devices are 32-bit elements; how exact they have to be, the bound alone decides.
A program may use at most 64 MiB of HBM per device.

```python
import math
import jax
import jax.numpy as jnp
from jax import lax

ORB = 4
KS = 32
T_DEV = 2
K = 1024
TIMES = 64
N_TA = 32


def strengthened(values, key, source, target, shards_of, factor):
    owner, partner = [(jnp.arange(values.shape[dim]) // (values.shape[dim] // shards_of)).reshape([-1 if axis == dim else 1 for axis in range(values.ndim)]) for dim in (source, target)]
    chosen = jax.random.permutation(key, shards_of)[partner]
    strong = (owner == chosen) | (owner == (partner + shards_of // 2) % shards_of)
    return jnp.where(strong, factor * values, values)


def block_scale(rng, extent, shards, low, top_value):
    level, own = 1.0, jax.random.fold_in(rng, 6)
    for position, shards_of in shards:
        heights = jnp.exp(jax.random.uniform(jax.random.fold_in(own, position), (shards_of,), jnp.float32, low / len(shards), top_value / len(shards)))
        level = level * jnp.repeat(heights, extent[position] // shards_of).reshape([-1 if axis == position else 1 for axis in range(len(extent))])
    return level


def gaussian(own_key, dims, deviation, limit, pieces=(), kind=jnp.bfloat16):
    entries = jax.random.normal(own_key, dims, jnp.float32) * deviation
    if len(pieces) > 0:
        entries = block_scale(own_key, dims, pieces, -0.22, 0.18) * entries
    return jnp.clip(entries, min=-limit, max=limit).astype(kind)


def bell_draw_with(key, extent, spread, most, pieces, heavy, held_as=jnp.bfloat16):
    entries = spread * jax.random.normal(key, extent, jnp.float32)
    if pieces:
        entries = entries * block_scale(key, extent, pieces, -0.22, 0.18)
    return jnp.clip(strengthened(entries, jax.random.fold_in(key, 3), *heavy), -most, most).astype(held_as)


def setup_inputs(seed: int = 0) -> dict:
    keys = jax.random.split(jax.random.key(seed), 9)
    return {
        "green_row": gaussian(keys[0], (2, ORB, ORB, TIMES, K), 1.0, 6.0, ((3, 32), (4, 8)), jnp.float32),
        "screen_lesser": gaussian(keys[1], (2, ORB, ORB, TIMES, K), 1.0, 6.0, ((3, 32), (4, 8)), jnp.float32),
        "screen_retarded": gaussian(keys[2], (2, ORB, ORB, TIMES, K), 1.0, 6.0, ((3, 32), (4, 8)), jnp.float32),
        "onsite": gaussian(keys[3], (2, ORB, ORB), 0.5, 3.0, (), jnp.float32),
        "lesser_slab": bell_draw_with(keys[4], (2, ORB, ORB, TIMES, TIMES, K), (2 * ORB * TIMES) ** -0.5, 0.5, ((3, 32), (5, 8)), (3, 4, 32, 2.75)),
        "advanced_slab": bell_draw_with(keys[5], (2, ORB, ORB, TIMES, TIMES, K), (2 * ORB * TIMES) ** -0.5, 0.5, ((3, 32), (5, 8)), (3, 4, 32, 2.75)),
        "slab_start": jax.random.randint(keys[6], (1,), 0, 4096).astype(jnp.int32),
        "block_table": jax.random.permutation(keys[7], N_TA).astype(jnp.int32),
    }


time_step = 0.1
drive_amp = 1.0
drive_freq = 0.37
highest = lax.Precision.HIGHEST

def phase_table(row_ids, col_ids, sign_value):
    products = row_ids[:, None] * col_ids[None, :] % KS
    angle = products.astype(jnp.float32) * (2.0 * math.pi / KS)
    factor = 1.0 / math.sqrt(KS)
    return (jnp.cos(angle) * factor, sign_value * jnp.sin(angle) * factor)

def along_last(values_in, cosine, sine_part):
    real_part = jnp.einsum('...m,mn->...n', values_in[0], cosine, precision=highest) - jnp.einsum('...m,mn->...n', values_in[1], sine_part, precision=highest)
    imag_part = jnp.einsum('...m,mn->...n', values_in[0], sine_part, precision=highest) + jnp.einsum('...m,mn->...n', values_in[1], cosine, precision=highest)
    return jnp.stack([real_part, imag_part])

def along_second(values_in, cosine, sine_part):
    real_part = jnp.einsum('...mj,mn->...nj', values_in[0], cosine, precision=highest) - jnp.einsum('...mj,mn->...nj', values_in[1], sine_part, precision=highest)
    imag_part = jnp.einsum('...mj,mn->...nj', values_in[0], sine_part, precision=highest) + jnp.einsum('...mj,mn->...nj', values_in[1], cosine, precision=highest)
    return jnp.stack([real_part, imag_part])

def transform(values_in, sign_value):
    full_shape = values_in.shape
    grid = values_in.reshape(full_shape[:-1] + (KS, KS))
    numbers = jnp.arange(KS, dtype=jnp.int32)
    cosine, sine_part = phase_table(numbers, numbers, sign_value)
    grid = along_last(grid, cosine, sine_part)
    grid = along_second(grid, cosine, sine_part)
    return grid.reshape(full_shape)

def self_energy(row_space, screens):
    green_real = row_space[0][None]
    green_imag = row_space[1][None]
    real_part = -(green_real * screens[1] + green_imag * screens[0])
    imag_part = green_real * screens[0] - green_imag * screens[1]
    return jnp.stack([real_part, imag_part])

def coupling(sigma_pair):
    return jnp.stack([jnp.stack([sigma_pair[0], -sigma_pair[1]]), jnp.stack([sigma_pair[1], sigma_pair[0]])])

def dispersion(slab_start, kx_ids, ky_ids):
    current = (slab_start[0] + TIMES).astype(jnp.float32)
    shift = drive_amp * jnp.sin(drive_freq * current)
    factor = 2.0 * math.pi / KS
    return -2.0 * (jnp.cos(kx_ids.astype(jnp.float32) * factor + shift) + jnp.cos(ky_ids.astype(jnp.float32) * factor))

def apply_h(row, onsite, energy):
    real_part = jnp.einsum('ab,bctk->actk', onsite[0], row[0], precision=highest) - jnp.einsum('ab,bctk->actk', onsite[1], row[1], precision=highest) + energy * row[0]
    imag_part = jnp.einsum('ab,bctk->actk', onsite[0], row[1], precision=highest) + jnp.einsum('ab,bctk->actk', onsite[1], row[0], precision=highest) + energy * row[1]
    return jnp.stack([real_part, imag_part])

def collide(ret_coupling, less_coupling, lesser_slab, advanced_slab, causal):
    block = math.gcd(K, 128)

    def one_block(counter):
        begin = counter * block
        part_ret = lax.dynamic_slice_in_dim(ret_coupling, begin, block, 5).astype(jnp.float32)
        part_less = lax.dynamic_slice_in_dim(less_coupling, begin, block, 5).astype(jnp.float32)
        slab_one = lax.dynamic_slice_in_dim(lesser_slab, begin, block, 5).astype(jnp.float32)
        slab_two = lax.dynamic_slice_in_dim(advanced_slab, begin, block, 5).astype(jnp.float32) * causal[:, :, None]
        return jnp.einsum('pqabsk,qbcstk->pactk', part_ret, slab_one) + jnp.einsum('pqabsk,qbcstk->pactk', part_less, slab_two)
    blocks = lax.map(one_block, jnp.arange(K // block, dtype=jnp.int32))
    return jnp.moveaxis(blocks, 0, -2).reshape((2, ORB, ORB, TIMES, K))

def reference(green_row, screen_lesser, screen_retarded, onsite, lesser_slab, advanced_slab, slab_start, block_table):
    offsets = jnp.arange(TIMES, dtype=jnp.int32)
    times_abs = jnp.repeat(block_table, T_DEV) * T_DEV + offsets % T_DEV
    causal = (times_abs[:, None] <= times_abs[None, :]).astype(jnp.float32)
    momenta = jnp.arange(K, dtype=jnp.int32)
    energy = dispersion(slab_start, momenta // KS, momenta % KS)
    screens = transform(jnp.stack([screen_lesser, screen_retarded], axis=1), 1.0)

    def rate_of(row):
        row_space = transform(row, 1.0)
        sigma_all = transform(self_energy(row_space, screens), -1.0).astype(jnp.bfloat16)
        collision = collide(coupling(sigma_all[:, 1]), coupling(sigma_all[:, 0]), lesser_slab, advanced_slab, causal)
        totals = apply_h(row, onsite, energy) + collision
        return jnp.stack([totals[1], -totals[0]])
    first_rate = rate_of(green_row)
    estimate = green_row + time_step * first_rate
    latest = first_rate
    for corrector in range(2):
        latest = rate_of(estimate)
        estimate = green_row + 0.5 * time_step * (first_rate + latest)
    return (estimate, latest)
```

```python
import math

import jax
import jax.numpy as jnp
import numpy as np
from jax import lax
from jax.experimental import pallas as pl
from jax.experimental.pallas import tpu as pltpu
from jax.sharding import PartitionSpec as P

KS = 32
MESH = pl.DeviceIdType.MESH
F32 = jnp.float32
BF16 = jnp.bfloat16

time_step = 0.1
drive_amp = 1.0
drive_freq = 0.37


def split_np(x):
    hi = x.astype(np.float32).astype(jnp.bfloat16)
    lo = (x - hi.astype(np.float64)).astype(np.float32).astype(jnp.bfloat16)
    return hi, lo


def tables():
    ka, x1 = np.meshgrid(np.arange(8), np.arange(8), indexing="ij")
    c8, s8 = np.cos(2 * np.pi * ka * x1 / 8), np.sin(2 * np.pi * ka * x1 / 8)
    eye = np.eye(4)
    fwd = np.zeros((2, 8, 4, 8, 2, 4))
    bwd = np.zeros((8, 2, 4, 2, 8, 4))
    for k in range(8):
        for x in range(8):
            c, s = c8[k, x] * eye / KS, s8[k, x] * eye / KS
            fwd[0, x, :, k, 0, :] = c
            fwd[0, x, :, k, 1, :] = -s
            fwd[1, x, :, k, 0, :] = s
            fwd[1, x, :, k, 1, :] = c
            bwd[k, 0, :, 0, x, :] = c
            bwd[k, 0, :, 1, x, :] = s
            bwd[k, 1, :, 0, x, :] = -s
            bwd[k, 1, :, 1, x, :] = c
    left = []
    for m in (fwd.reshape(64, 64), bwd.reshape(64, 64)):
        hi, lo = split_np(m)
        left.append(np.concatenate([hi, lo, hi], axis=1))
    left = np.stack(left)
    lane = np.arange(128)
    j, y = lane // 32, lane % 32
    angle = 2 * np.pi * (np.outer(j, j) / 4 + np.outer(y, y) / 32)
    c, s = np.cos(angle), np.sin(angle)
    right = []
    for m in (np.block([[c, s], [-s, c]]), np.block([[c, -s], [s, c]])):
        right.extend(split_np(m))
    right = np.stack(right)
    row = np.arange(32) // 4
    tw = 2 * np.pi * np.outer(row, j) / 32
    twiddle = np.stack([np.cos(tw), np.sin(tw)]).astype(np.float32)
    return left, right, twiddle


def split(x):
    hi = x.astype(BF16)
    lo = (x - hi.astype(F32)).astype(BF16)
    return hi, lo


def mm(a, b):
    return jnp.dot(a, b, preferred_element_type=F32)


def left_product(table, x):
    hi, lo = split(x)
    return mm(table, jnp.concatenate([hi, hi, lo], axis=0))


def right_product(hi_table, lo_table, x):
    rows = x.shape[0]
    hi, lo = split(x)
    both = mm(jnp.concatenate([hi, lo], axis=0), hi_table)
    return both[:rows] + both[rows:] + mm(hi, lo_table)


def order(i):
    half = (i + 1) // 2
    return 4 + half - 2 * half * (i % 2)


def kernel(
    onsite, table, green, less, ret, energy, adv_hbm, les_hbm, left, right, twiddle,
    next_row, derivative,
    raw, slab, isend, irecv, gsend, grecv, screens, ssend, srecv, sig,
    out_o, cown, crecv, ysend, yrecv, zsend, zrecv,
    gbuf, hg, first,
    raw_sem, is_sem, ir_sem, gs_sem, gr_sem, ss_sem, sr_sem,
    cs_sem, cr_sem, ys_sem, yr_sem, zs_sem, zr_sem,
):
    ta, ka = lax.axis_index("ta"), lax.axis_index("ka")
    z, y, core = ta // 4, (ta // 2) % 2, ta % 2
    sibling = ta + 1 - 2 * core
    across = ta + 2 - 4 * y

    adv_copy = pltpu.make_async_copy(adv_hbm, raw.at[0], raw_sem.at[0])
    les_copy = pltpu.make_async_copy(les_hbm, raw.at[1], raw_sem.at[1])
    adv_copy.start()
    les_copy.start()

    barrier = pltpu.get_barrier_semaphore()
    for i in range(1, 8):
        pl.semaphore_signal(barrier, inc=1, device_id=(ta, (ka + i) % 8), device_id_type=MESH)
        pl.semaphore_signal(barrier, inc=1, device_id=((ta + 4 * i) % 32, ka), device_id_type=MESH)
    pl.semaphore_signal(barrier, inc=1, device_id=(sibling, ka), device_id_type=MESH)
    pl.semaphore_signal(barrier, inc=1, device_id=(across, ka), device_id_type=MESH)

    for n, ref in enumerate((less, ret, green)):
        for d in range(8):
            isend[d, 8 * n : 8 * n + 8, :] = ref[pl.ds(d, 8, stride=8), :]
    gbuf[...] = green[...]
    pl.semaphore_wait(barrier, 16)

    sends = []

    def push(src, dst, ssem, rsem, to):
        copy = pltpu.make_async_remote_copy(
            src_ref=src, dst_ref=dst, send_sem=ssem, recv_sem=rsem,
            device_id=to, device_id_type=MESH,
        )
        copy.start()
        return copy

    def arrived(dst, rsem):
        pltpu.make_async_remote_copy(
            src_ref=dst, dst_ref=dst, send_sem=rsem, recv_sem=rsem,
            device_id=(ta, ka), device_id_type=MESH,
        ).wait_recv()

    def exchange(src, dst, ssem, rsem):
        for i in range(1, 8):
            peer = (ka + i) % 8
            sends.append(push(src.at[peer], dst.at[ka], ssem.at[i], rsem.at[ka], (ta, peer)))
        dst[ka] = src[ka]

    def collect(dst, rsem):
        for i in range(1, 8):
            peer = (ka + i) % 8
            arrived(dst.at[peer], rsem.at[peer])

    exchange(isend, irecv, is_sem, ir_sem)

    row = lax.broadcasted_iota(jnp.int32, (256, 256), 0)
    col = lax.broadcasted_iota(jnp.int32, (256, 256), 1)
    place = row // 8
    source = (
        ((row // 2) % 4) * 64 + (place % 8) * 8 + ((place // 8) % 2) * 4 + (place // 16) * 2 + row % 2
    )
    picked = source == col
    lane = lax.broadcasted_iota(jnp.int32, (1, 256), 1) % 64
    tau = jnp.zeros((1, 256), jnp.int32)
    for i in range(32):
        tau = jnp.where(lane // 2 == i, 2 * table[i], tau)
    tau = tau + lane % 2
    own = 2 * table[ta]
    plain = jnp.where(picked, 1.0, 0.0).astype(BF16)
    masked = [
        jnp.where(picked & (own + s <= tau), 1.0, 0.0).astype(BF16) for s in range(2)
    ]
    adv_copy.wait()
    les_copy.wait()

    def relay(b, carry):
        for kind in range(2):
            for s in range(2):
                parts = [
                    jnp.concatenate([raw[kind, q, b, c, s] for c in range(4)], axis=0)
                    for q in range(2)
                ]
                moved = mm(masked[s] if kind == 0 else plain, jnp.concatenate(parts, axis=1))
                re, im = moved[:, :128], moved[:, 128:]
                d = b * 2 + s
                slab[kind, 0, d] = re.reshape(32, 8, 128)
                slab[kind, 1, d] = im.reshape(32, 8, 128)
                slab[kind, 2, d] = (re + im).reshape(32, 8, 128)
        return carry

    lax.fori_loop(0, 4, relay, 0)

    tw_c, tw_s = twiddle[0], twiddle[1]

    def to_space(tiles):
        mixed = left_product(left[0], tiles)
        n = tiles.shape[1] // 128
        turned = []
        for i in range(n):
            re, im = (mixed[32 * p : 32 * p + 32, 128 * i : 128 * i + 128] for p in range(2))
            turned.append(
                jnp.concatenate([re * tw_c - im * tw_s, re * tw_s + im * tw_c], axis=1)
            )
        out = right_product(right[0], right[1], jnp.concatenate(turned, axis=0))
        return [out[32 * i : 32 * i + 32] for i in range(n)]

    def to_momenta(fields):
        out = right_product(right[2], right[3], jnp.concatenate(fields, axis=0))
        turned = []
        for i in range(2):
            re, im = out[32 * i : 32 * i + 32, :128], out[32 * i : 32 * i + 32, 128:]
            turned.append(
                jnp.concatenate([re * tw_c + im * tw_s, im * tw_c - re * tw_s], axis=0)
            )
        return left_product(left[1], jnp.concatenate(turned, axis=1))

    collect(irecv, ir_sem)
    tiles = jnp.concatenate(
        [irecv[:, 8 * n : 8 * n + 8, :].reshape(64, 128) for n in range(3)], axis=1
    )
    w_less, w_ret, space = to_space(tiles)
    screens[0] = w_less
    screens[1] = w_ret

    def blocks(group, i0):
        js = [group * 8 + (z + order(i0 + n)) % 8 for n in range(2)]
        acc = [[[None] * 3 for _ in range(4)] for _ in range(2)]
        for kind in range(2):
            for d in range(8):
                for q in range(3):
                    values = [slab[kind, q, d, js[n]] for n in range(2)]
                    for a in range(4):
                        factor = sig[kind, q, d, a]
                        for n in range(2):
                            term = factor * values[n]
                            old = acc[n][a][q]
                            acc[n][a][q] = term if old is None else old + term
        out = []
        for n in range(2):
            re = [acc[n][a][0] - acc[n][a][1] for a in range(4)]
            im = [acc[n][a][2] - acc[n][a][0] - acc[n][a][1] for a in range(4)]
            out.append(re + im)
        return out

    def reduced(r):
        def for_sibling(half, group):
            def body(piece, carry):
                out = blocks(group, 2 * piece)
                for n in range(2):
                    for m in range(8):
                        out_o[r, half, 2 * piece + n, m] = out[n][m]
                push(
                    out_o.at[r, half, pl.ds(2 * piece, 2)], crecv.at[r, half, pl.ds(2 * piece, 2)],
                    cs_sem.at[r, half, piece], cr_sem.at[r, half, piece], (sibling, ka),
                )
                return carry

            lax.fori_loop(0, 4, body, 0)

        def from_sibling(half, piece):
            arrived(crecv.at[r, half, pl.ds(2 * piece, 2)], cr_sem.at[r, half, piece])

        for_sibling(0, (1 - core) * 2 + 1 - y)

        def to_across(piece, carry):
            out = blocks(core * 2 + 1 - y, 2 * piece)
            from_sibling(0, piece)
            for n in range(2):
                for m in range(8):
                    ysend[r, 2 * piece + n, m] = out[n][m] + crecv[r, 0, 2 * piece + n, m]
            push(
                ysend.at[r, pl.ds(2 * piece, 2)], yrecv.at[r, pl.ds(2 * piece, 2)],
                ys_sem.at[r, piece], yr_sem.at[r, piece], (across, ka),
            )
            return carry

        lax.fori_loop(0, 4, to_across, 0)
        for_sibling(1, (1 - core) * 2 + y)

        def mine(piece, carry):
            out = blocks(core * 2 + y, 2 * piece)
            from_sibling(1, piece)
            for n in range(2):
                for m in range(8):
                    cown[2 * piece + n, m] = out[n][m] + crecv[r, 1, 2 * piece + n, m]
            return carry

        lax.fori_loop(0, 4, mine, 0)

        for i in range(8):
            if i % 2 == 0:
                arrived(yrecv.at[r, pl.ds(i, 2)], yr_sem.at[r, i // 2])
            zsend[r, i] = cown[i] + yrecv[r, i]
            if i < 7:
                away = (z + order(i)) % 8
                sends.append(
                    push(
                        zsend.at[r, i], zrecv.at[r, z], zs_sem.at[r, i], zr_sem.at[r, z],
                        (away * 4 + ta % 4, ka),
                    )
                )
        total = zsend[r, 7]
        for i in range(1, 8):
            peer = (z + i) % 8
            arrived(zrecv.at[r, peer], zr_sem.at[r, peer])
            total = total + zrecv[r, peer]
        for half in range(2):
            for piece in range(4):
                pltpu.make_async_remote_copy(
                    src_ref=out_o.at[r, half, pl.ds(2 * piece, 2)],
                    dst_ref=crecv.at[r, half, pl.ds(2 * piece, 2)],
                    send_sem=cs_sem.at[r, half, piece], recv_sem=cr_sem.at[r, half, piece],
                    device_id=(sibling, ka), device_id_type=MESH,
                ).wait_send()
        for piece in range(4):
            pltpu.make_async_remote_copy(
                src_ref=ysend.at[r, pl.ds(2 * piece, 2)], dst_ref=yrecv.at[r, pl.ds(2 * piece, 2)],
                send_sem=ys_sem.at[r, piece], recv_sem=yr_sem.at[r, piece],
                device_id=(across, ka), device_id_type=MESH,
            ).wait_send()
        return total

    for r in range(3):
        if r > 0:
            for d in range(8):
                gsend[r - 1, d] = gbuf[pl.ds(d, 8, stride=8), :]
            exchange(gsend.at[r - 1], grecv.at[r - 1], gs_sem.at[r - 1], gr_sem.at[r - 1])
            collect(grecv.at[r - 1], gr_sem.at[r - 1])
            (space,) = to_space(grecv[r - 1].reshape(64, 128))
        re, im = space[:, :128], space[:, 128:]
        fields = []
        for kind in range(2):
            w_re, w_im = screens[kind, :, :128], screens[kind, :, 128:]
            fields.append(
                jnp.concatenate([-(re * w_im + im * w_re), re * w_re - im * w_im], axis=1)
            )
        sigma = to_momenta(fields)
        for kind in range(2):
            ssend[r, :, kind] = sigma[:, 128 * kind : 128 * kind + 128].reshape(8, 8, 128)
        exchange(ssend.at[r], srecv.at[r], ss_sem.at[r], sr_sem.at[r])

        e = energy[...]
        rows = [gbuf[8 * m : 8 * m + 8] for m in range(8)]
        for a in range(4):
            re, im = e * rows[a], e * rows[4 + a]
            for b in range(4):
                o_re, o_im = onsite[4 * a + b], onsite[16 + 4 * a + b]
                re = re + o_re * rows[b] - o_im * rows[4 + b]
                im = im + o_re * rows[4 + b] + o_im * rows[b]
            hg[a] = re
            hg[4 + a] = im

        collect(srecv.at[r], sr_sem.at[r])
        for kind in range(2):
            for d in range(8):
                tile = srecv[r, d, kind].astype(BF16).astype(F32)
                for a in range(4):
                    s_re = jnp.broadcast_to(tile[a : a + 1], (8, 128))
                    s_im = jnp.broadcast_to(tile[4 + a : 5 + a], (8, 128))
                    sig[kind, 0, d, a] = s_re
                    sig[kind, 1, d, a] = s_im
                    sig[kind, 2, d, a] = s_re + s_im

        total = reduced(r) + hg[...]
        rate = jnp.concatenate([total[4:], -total[:4]], axis=0).reshape(64, 128)
        if r == 0:
            first[...] = rate
            gbuf[...] = green[...] + time_step * rate
        elif r == 1:
            gbuf[...] = green[...] + (0.5 * time_step) * (first[...] + rate)
        else:
            next_row[...] = green[...] + (0.5 * time_step) * (first[...] + rate)
            derivative[...] = rate

    for copy in sends:
        copy.wait_send()


def dispersion(slab_start, all_times, kx_ids, ky_ids):
    current = (slab_start[0] + all_times).astype(jnp.float32)
    shift = drive_amp * jnp.sin(drive_freq * current)
    factor = 2.0 * math.pi / KS
    return -2.0 * (
        jnp.cos(kx_ids.astype(jnp.float32) * factor + shift)
        + jnp.cos(ky_ids.astype(jnp.float32) * factor)
    )


def local(
    green_row, screen_lesser, screen_retarded, onsite, lesser_slab, advanced_slab, slab_start,
    block_table,
):
    k_local = green_row.shape[4]
    ka_index = lax.axis_index("ka")
    momenta = ka_index * k_local + jnp.arange(k_local, dtype=jnp.int32)
    energy = dispersion(slab_start, 64, momenta // KS, momenta % KS).reshape(1, k_local)
    left, right, twiddle = tables()

    def vmem():
        return pl.BlockSpec(memory_space=pltpu.VMEM)

    def smem():
        return pl.BlockSpec(memory_space=pltpu.SMEM)

    def scratch(*dims, kind=F32):
        return pltpu.VMEM(dims, kind)

    def sems(*dims):
        return pltpu.SemaphoreType.DMA(dims)

    rows = jax.ShapeDtypeStruct((64, 128), F32)
    next_row, derivative = pl.pallas_call(
        kernel,
        name="gw_step",
        out_shape=(rows, rows),
        in_specs=[smem(), smem()] + [vmem()] * 4 + [pl.BlockSpec(memory_space=pl.ANY)] * 2
        + [vmem()] * 3,
        out_specs=(vmem(), vmem()),
        scratch_shapes=[
            scratch(2, 2, 4, 4, 2, 64, 128, kind=BF16),
            scratch(2, 3, 8, 32, 8, 128),
            scratch(8, 24, 128),
            scratch(8, 24, 128),
            scratch(2, 8, 8, 128),
            scratch(2, 8, 8, 128),
            scratch(2, 32, 256),
            scratch(3, 8, 2, 8, 128),
            scratch(3, 8, 2, 8, 128),
            scratch(2, 3, 8, 4, 8, 128),
            scratch(3, 2, 8, 8, 8, 128),
            scratch(8, 8, 8, 128),
            scratch(3, 2, 8, 8, 8, 128),
            scratch(3, 8, 8, 8, 128),
            scratch(3, 8, 8, 8, 128),
            scratch(3, 8, 8, 8, 128),
            scratch(3, 8, 8, 8, 128),
            scratch(64, 128),
            scratch(8, 8, 128),
            scratch(64, 128),
            sems(2),
            sems(8), sems(8),
            sems(2, 8), sems(2, 8),
            sems(3, 8), sems(3, 8),
            sems(3, 2, 4), sems(3, 2, 4),
            sems(3, 4), sems(3, 4),
            sems(3, 8), sems(3, 8),
        ],
        compiler_params=pltpu.CompilerParams(
            collective_id=0, has_side_effects=True, vmem_limit_bytes=48 * 2**20
        ),
    )(
        onsite.reshape(32),
        block_table,
        green_row.reshape(64, 128),
        screen_lesser.reshape(64, 128),
        screen_retarded.reshape(64, 128),
        energy,
        advanced_slab,
        lesser_slab,
        jnp.asarray(left),
        jnp.asarray(right),
        jnp.asarray(twiddle),
    )
    return next_row.reshape(green_row.shape), derivative.reshape(green_row.shape)


def solution(mesh):
    return jax.shard_map(
        local,
        mesh=mesh,
        in_specs=(
            P(None, None, None, "ta", "ka"),
            P(None, None, None, "ta", "ka"),
            P(None, None, None, "ta", "ka"),
            P(),
            P(None, None, None, "ta", None, "ka"),
            P(None, None, None, "ta", None, "ka"),
            P(),
            P(),
        ),
        out_specs=(P(None, None, None, "ta", "ka"), P(None, None, None, "ta", "ka")),
        check_vma=False,
    )
```

```python
import math

import jax
import jax.numpy as jnp
import numpy as np
from jax import lax
from jax.experimental import pallas as pl
from jax.experimental.pallas import tpu as pltpu
from jax.sharding import PartitionSpec as P

KS = 32
MESH = pl.DeviceIdType.MESH
F32 = jnp.float32
BF16 = jnp.bfloat16

time_step = 0.1
drive_amp = 1.0
drive_freq = 0.37


def split_np(x):
    hi = x.astype(np.float32).astype(jnp.bfloat16)
    lo = (x - hi.astype(np.float64)).astype(np.float32).astype(jnp.bfloat16)
    return hi, lo


def tables():
    ka, x1 = np.meshgrid(np.arange(8), np.arange(8), indexing="ij")
    c8, s8 = np.cos(2 * np.pi * ka * x1 / 8), np.sin(2 * np.pi * ka * x1 / 8)
    eye = np.eye(4)
    fwd = np.zeros((2, 8, 4, 8, 2, 4))
    bwd = np.zeros((8, 2, 4, 2, 8, 4))
    for k in range(8):
        for x in range(8):
            c, s = c8[k, x] * eye / KS, s8[k, x] * eye / KS
            fwd[0, x, :, k, 0, :] = c
            fwd[0, x, :, k, 1, :] = -s
            fwd[1, x, :, k, 0, :] = s
            fwd[1, x, :, k, 1, :] = c
            bwd[k, 0, :, 0, x, :] = c
            bwd[k, 0, :, 1, x, :] = s
            bwd[k, 1, :, 0, x, :] = -s
            bwd[k, 1, :, 1, x, :] = c
    left = []
    for m in (fwd.reshape(64, 64), bwd.reshape(64, 64)):
        hi, lo = split_np(m)
        left.append(np.concatenate([hi, lo, hi], axis=1))
    left = np.stack(left)
    lane = np.arange(128)
    j, y = lane // 32, lane % 32
    angle = 2 * np.pi * (np.outer(j, j) / 4 + np.outer(y, y) / 32)
    c, s = np.cos(angle), np.sin(angle)
    right = []
    for m in (np.block([[c, s], [-s, c]]), np.block([[c, -s], [s, c]])):
        right.extend(split_np(m))
    right = np.stack(right)
    row = np.arange(32) // 4
    tw = 2 * np.pi * np.outer(row, j) / 32
    twiddle = np.stack([np.cos(tw), np.sin(tw)]).astype(np.float32)
    return left, right, twiddle


def split(x):
    hi = x.astype(BF16)
    lo = (x - hi.astype(F32)).astype(BF16)
    return hi, lo


def mm(a, b):
    return jnp.dot(a, b, preferred_element_type=F32)


def left_product(table, x):
    hi, lo = split(x)
    return mm(table, jnp.concatenate([hi, hi, lo], axis=0))


def right_product(hi_table, lo_table, x):
    rows = x.shape[0]
    hi, lo = split(x)
    both = mm(jnp.concatenate([hi, lo], axis=0), hi_table)
    return both[:rows] + both[rows:] + mm(hi, lo_table)


def order(i):
    half = (i + 1) // 2
    return 4 + half - 2 * half * (i % 2)


def kernel(
    onsite_hbm, table_hbm, begin_hbm, green_hbm, less_hbm, ret_hbm, adv_hbm, les_hbm,
    left_hbm, right_hbm, twiddle_hbm,
    next_row, derivative,
    onsite, table, begin, green, less, ret, left, right, twiddle,
    raw, slab, oslab, isend, irecv, gsend, grecv, screens, ssend, srecv, sig,
    own, ysend, yrecv, zsend, zrecv, gbuf, hg, first,
    in_sem, os_sem, or_sem, is_sem, ir_sem, gs_sem, gr_sem, ss_sem, sr_sem,
    ys_sem, yr_sem, zs_sem, zr_sem,
):
    ta, ka = lax.axis_index("ta"), lax.axis_index("ka")
    z, y, core = ta // 4, (ta // 2) % 2, ta % 2
    sibling = ta + 1 - 2 * core
    across = ta + 2 - 4 * y

    loads = [
        pltpu.make_async_copy(src, dst, in_sem.at[i])
        for i, (src, dst) in enumerate(
            (
                (less_hbm, less), (ret_hbm, ret), (green_hbm, green), (table_hbm, table),
                (adv_hbm, raw.at[0]), (les_hbm, raw.at[1]), (onsite_hbm, onsite),
                (begin_hbm, begin), (left_hbm, left), (right_hbm, right), (twiddle_hbm, twiddle),
            )
        )
    ]
    for copy in loads:
        copy.start()

    barrier = pltpu.get_barrier_semaphore()
    for i in range(1, 8):
        pl.semaphore_signal(barrier, inc=1, device_id=(ta, (ka + i) % 8), device_id_type=MESH)
        pl.semaphore_signal(barrier, inc=1, device_id=(sibling, (ka + i) % 8), device_id_type=MESH)
        pl.semaphore_signal(barrier, inc=1, device_id=((ta + 4 * i) % 32, ka), device_id_type=MESH)
    pl.semaphore_signal(barrier, inc=1, device_id=(sibling, ka), device_id_type=MESH)
    pl.semaphore_signal(barrier, inc=1, device_id=(across, ka), device_id_type=MESH)

    row = lax.broadcasted_iota(jnp.int32, (256, 1), 0)
    col = lax.broadcasted_iota(jnp.int32, (256, 256), 1)
    place = row // 8
    source = (
        ((row // 2) % 4) * 64 + (place % 8) * 8 + ((place // 8) % 2) * 4
        + ((core + place // 16) % 2) * 2 + row % 2
    )
    picked = source == col
    lane = lax.broadcasted_iota(jnp.int32, (1, 256), 1) % 64
    for copy in loads[:4]:
        copy.wait()
    for n, ref in enumerate((less, ret, green)):
        for d in range(8):
            isend[d, 8 * n : 8 * n + 8, :] = ref[pl.ds(d, 8, stride=8), :]
    gbuf[...] = green[...]
    tau = jnp.zeros((1, 256), jnp.int32)
    for i in range(32):
        tau = jnp.where(lane // 2 == i, 2 * table[i], tau)
    tau = tau + lane % 2
    now = 2 * table[ta]
    plain = jnp.where(picked, 1.0, 0.0).astype(BF16)
    masked = [
        jnp.where(picked & (now + s <= tau), 1.0, 0.0).astype(BF16) for s in range(2)
    ]
    for copy in loads[4:]:
        copy.wait()

    def relay(b, carry):
        for kind in range(2):
            for s in range(2):
                parts = [
                    jnp.concatenate([raw[kind, q, b, c, s] for c in range(4)], axis=0)
                    for q in range(2)
                ]
                moved = mm(masked[s] if kind == 0 else plain, jnp.concatenate(parts, axis=1))
                re, im = moved[:, :128], moved[:, 128:]
                d = b * 2 + s
                slab[kind, 0, core * 8 + d] = re[:128].reshape(16, 8, 128)
                slab[kind, 1, core * 8 + d] = im[:128].reshape(16, 8, 128)
                slab[kind, 2, core * 8 + d] = (re[:128] + im[:128]).reshape(16, 8, 128)
                oslab[kind, 0, d] = re[128:].reshape(16, 8, 128)
                oslab[kind, 1, d] = im[128:].reshape(16, 8, 128)
        return carry

    lax.fori_loop(0, 4, relay, 0)

    pl.semaphore_wait(barrier, 23)

    def describe(src, dst, ssem, rsem, to):
        return pltpu.make_async_remote_copy(
            src_ref=src, dst_ref=dst, send_sem=ssem, recv_sem=rsem,
            device_id=to, device_id_type=MESH,
        )

    def push(src, dst, ssem, rsem, to):
        describe(src, dst, ssem, rsem, to).start()

    def arrived(dst, rsem):
        describe(dst, dst, rsem, rsem, (sibling, ka)).wait_recv()

    def sent(src, ssem):
        describe(src, src, ssem, ssem, (sibling, ka)).wait_send()

    def exchange(src, dst, ssem, rsem):
        for i in range(7, 0, -1):
            peer = (ka + i) % 8
            push(src.at[peer], dst.at[ka], ssem.at[i], rsem.at[ka], (ta, peer))
        dst[ka] = src[ka]

    def collect(dst, rsem):
        for i in range(1, 8):
            peer = (ka + i) % 8
            arrived(dst.at[peer], rsem.at[peer])

    exchange(isend, irecv, is_sem, ir_sem)
    for kind in range(2):
        for q in range(2):
            push(
                oslab.at[kind, q], slab.at[kind, q, pl.ds(core * 8, 8)],
                os_sem.at[kind, q], or_sem.at[kind, q], (sibling, ka),
            )

    shift = drive_amp * jnp.sin(
        jnp.full((8, 128), drive_freq, F32) * (begin[0] + 64).astype(F32)
    )
    k_lane = lax.broadcasted_iota(jnp.int32, (8, 128), 1)
    factor = 2.0 * math.pi / KS
    e = -2.0 * (
        jnp.cos((4 * ka + k_lane // KS).astype(F32) * factor + shift)
        + jnp.cos((k_lane % KS).astype(F32) * factor)
    )

    tw_c, tw_s = twiddle[0], twiddle[1]

    def to_space(tiles):
        mixed = left_product(left[0], tiles)
        n = tiles.shape[1] // 128
        turned = []
        for i in range(n):
            re, im = (mixed[32 * p : 32 * p + 32, 128 * i : 128 * i + 128] for p in range(2))
            turned.append(
                jnp.concatenate([re * tw_c - im * tw_s, re * tw_s + im * tw_c], axis=1)
            )
        out = right_product(right[0], right[1], jnp.concatenate(turned, axis=0))
        return [out[32 * i : 32 * i + 32] for i in range(n)]

    def to_momenta(fields):
        out = right_product(right[2], right[3], jnp.concatenate(fields, axis=0))
        turned = []
        for i in range(2):
            re, im = out[32 * i : 32 * i + 32, :128], out[32 * i : 32 * i + 32, 128:]
            turned.append(
                jnp.concatenate([re * tw_c + im * tw_s, im * tw_c - re * tw_s], axis=0)
            )
        return left_product(left[1], jnp.concatenate(turned, axis=1))

    collect(irecv, ir_sem)
    tiles = jnp.concatenate(
        [irecv[:, 8 * n : 8 * n + 8, :].reshape(64, 128) for n in range(3)], axis=1
    )
    w_less, w_ret, space = to_space(tiles)
    screens[0] = w_less
    screens[1] = w_ret

    def blocks(js):
        acc = [[[None] * 3 for _ in range(4)] for _ in range(2)]
        for kind in range(2):
            for sd in range(16):
                for q in range(3):
                    values = [slab[kind, q, sd, j] for j in js]
                    for a in range(4):
                        factor = sig[kind, q, sd, a]
                        for n in range(2):
                            term = factor * values[n]
                            old = acc[n][a][q]
                            acc[n][a][q] = term if old is None else old + term
        out = []
        for n in range(2):
            re = [acc[n][a][0] - acc[n][a][1] for a in range(4)]
            im = [acc[n][a][2] - acc[n][a][0] - acc[n][a][1] for a in range(4)]
            out.append(re + im)
        return out

    def reduced(r):
        def to_across(piece, carry):
            places = [(z + order(2 * piece + n)) % 8 for n in range(2)]
            out = blocks([(1 - y) * 8 + p for p in places])
            for n in range(2):
                i = 2 * piece + n
                for m in range(8):
                    ysend[r, i, m] = out[n][m]
                push(ysend.at[r, i], yrecv.at[r, i], ys_sem.at[r, i], yr_sem.at[r, i], (across, ka))
            return carry

        lax.fori_loop(0, 4, to_across, 0)

        def mine(piece, carry):
            places = [(z + order(2 * piece + n)) % 8 for n in range(2)]
            out = blocks([y * 8 + p for p in places])
            for n in range(2):
                for m in range(8):
                    own[2 * piece + n, m] = out[n][m]
            return carry

        lax.fori_loop(0, 4, mine, 0)

        for i in range(8):
            arrived(yrecv.at[r, i], yr_sem.at[r, i])
            if i < 7:
                zsend[r, i] = own[i] + yrecv[r, i]
                away = (z + order(i)) % 8
                push(
                    zsend.at[r, i], zrecv.at[r, z], zs_sem.at[r, i], zr_sem.at[r, z],
                    (away * 4 + ta % 4, ka),
                )
        total = own[7] + yrecv[r, 7] + hg[...]
        for i in range(7):
            peer = (z + order(i)) % 8
            arrived(zrecv.at[r, peer], zr_sem.at[r, peer])
            total = total + zrecv[r, peer]
        return total

    for r in range(3):
        if r > 0:
            for d in range(8):
                gsend[r - 1, d] = gbuf[pl.ds(d, 8, stride=8), :]
            exchange(gsend.at[r - 1], grecv.at[r - 1], gs_sem.at[r - 1], gr_sem.at[r - 1])

        rows = [gbuf[8 * m : 8 * m + 8] for m in range(8)]
        for a in range(4):
            re, im = e * rows[a], e * rows[4 + a]
            for b in range(4):
                o_re, o_im = onsite[0, a, b], onsite[1, a, b]
                re = re + o_re * rows[b] - o_im * rows[4 + b]
                im = im + o_re * rows[4 + b] + o_im * rows[b]
            hg[a] = re
            hg[4 + a] = im

        if r > 0:
            collect(grecv.at[r - 1], gr_sem.at[r - 1])
            (space,) = to_space(grecv[r - 1].reshape(64, 128))
        re, im = space[:, :128], space[:, 128:]
        fields = []
        for kind in range(2):
            w_re, w_im = screens[kind, :, :128], screens[kind, :, 128:]
            fields.append(
                jnp.concatenate([-(re * w_im + im * w_re), re * w_re - im * w_im], axis=1)
            )
        sigma = to_momenta(fields)
        for kind in range(2):
            ssend[r, :, kind] = sigma[:, 128 * kind : 128 * kind + 128].reshape(8, 8, 128)
        slot = core * 8 + ka
        for i in range(7, 0, -1):
            peer = (ka + i) % 8
            for n, to in enumerate((ta, sibling)):
                push(
                    ssend.at[r, peer], srecv.at[r, slot], ss_sem.at[r, 2 * i + n],
                    sr_sem.at[r, slot], (to, peer),
                )
        push(
            ssend.at[r, ka], srecv.at[r, slot], ss_sem.at[r, 0], sr_sem.at[r, slot], (sibling, ka)
        )
        srecv[r, slot] = ssend[r, ka]

        if r == 0:
            for kind in range(2):
                for q in range(2):
                    theirs = slab.at[kind, q, pl.ds((1 - core) * 8, 8)]
                    arrived(theirs, or_sem.at[kind, q])
                for d in range(8):
                    sd = (1 - core) * 8 + d
                    slab[kind, 2, sd] = slab[kind, 0, sd] + slab[kind, 1, sd]

        for i in range(8):
            peer = (ka + i) % 8
            for n in range(2):
                if i + n > 0:
                    sd = ((core + n) % 2) * 8 + peer
                    arrived(srecv.at[r, sd], sr_sem.at[r, sd])
        for sd in range(16):
            for kind in range(2):
                tile = srecv[r, sd, kind].astype(BF16).astype(F32)
                for a in range(4):
                    s_re = jnp.broadcast_to(tile[a : a + 1], (8, 128))
                    s_im = jnp.broadcast_to(tile[4 + a : 5 + a], (8, 128))
                    sig[kind, 0, sd, a] = s_re
                    sig[kind, 1, sd, a] = s_im
                    sig[kind, 2, sd, a] = s_re + s_im

        total = reduced(r)
        rate = jnp.concatenate([total[4:], -total[:4]], axis=0).reshape(64, 128)
        if r == 0:
            first[...] = rate
            gbuf[...] = green[...] + time_step * rate
        elif r == 1:
            gbuf[...] = green[...] + (0.5 * time_step) * (first[...] + rate)
        else:
            next_row[...] = green[...] + (0.5 * time_step) * (first[...] + rate)
            derivative[...] = rate

    for i in range(1, 8):
        sent(isend.at[(ka + i) % 8], is_sem.at[i])
    for kind in range(2):
        for q in range(2):
            sent(oslab.at[kind, q], os_sem.at[kind, q])
    for r in range(3):
        for i in range(1, 8):
            if r < 2:
                sent(gsend.at[r, (ka + i) % 8], gs_sem.at[r, i])
            for n in range(2):
                sent(ssend.at[r, (ka + i) % 8], ss_sem.at[r, 2 * i + n])
        sent(ssend.at[r, ka], ss_sem.at[r, 0])
        for i in range(8):
            sent(ysend.at[r, i], ys_sem.at[r, i])
            if i < 7:
                sent(zsend.at[r, i], zs_sem.at[r, i])


def local(
    green_row, screen_lesser, screen_retarded, onsite, lesser_slab, advanced_slab, slab_start,
    block_table,
):
    left, right, twiddle = tables()

    def hbm():
        return pl.BlockSpec(memory_space=pltpu.HBM)

    def vmem():
        return pl.BlockSpec(memory_space=pltpu.VMEM)

    def scratch(*dims, kind=F32):
        return pltpu.VMEM(dims, kind)

    def sems(*dims):
        return pltpu.SemaphoreType.DMA(dims)

    rows = jax.ShapeDtypeStruct((64, 128), F32)
    next_row, derivative = pl.pallas_call(
        kernel,
        name="gw_step",
        out_shape=(rows, rows),
        in_specs=[hbm()] * 11,
        out_specs=(vmem(), vmem()),
        scratch_shapes=[
            pltpu.SMEM((2, 4, 4), F32),
            pltpu.SMEM((32,), jnp.int32),
            pltpu.SMEM((1,), jnp.int32),
            scratch(64, 128),
            scratch(64, 128),
            scratch(64, 128),
            scratch(2, 64, 192, kind=BF16),
            scratch(4, 256, 256, kind=BF16),
            scratch(2, 32, 128),
            scratch(2, 2, 4, 4, 2, 64, 128, kind=BF16),
            scratch(2, 3, 16, 16, 8, 128),
            scratch(2, 2, 8, 16, 8, 128),
            scratch(8, 24, 128),
            scratch(8, 24, 128),
            scratch(2, 8, 8, 128),
            scratch(2, 8, 8, 128),
            scratch(2, 32, 256),
            scratch(3, 8, 2, 8, 128),
            scratch(3, 16, 2, 8, 128),
            scratch(2, 3, 16, 4, 8, 128),
            scratch(8, 8, 8, 128),
            scratch(3, 8, 8, 8, 128),
            scratch(3, 8, 8, 8, 128),
            scratch(3, 7, 8, 8, 128),
            scratch(3, 8, 8, 8, 128),
            scratch(64, 128),
            scratch(8, 8, 128),
            scratch(64, 128),
            sems(11),
            sems(2, 2), sems(2, 2),
            sems(8), sems(8),
            sems(2, 8), sems(2, 8),
            sems(3, 16), sems(3, 16),
            sems(3, 8), sems(3, 8),
            sems(3, 7), sems(3, 8),
        ],
        compiler_params=pltpu.CompilerParams(
            collective_id=0, has_side_effects=True, vmem_limit_bytes=56 * 2**20
        ),
    )(
        onsite,
        block_table,
        slab_start,
        green_row.reshape(64, 128),
        screen_lesser.reshape(64, 128),
        screen_retarded.reshape(64, 128),
        advanced_slab,
        lesser_slab,
        jnp.asarray(left),
        jnp.asarray(right),
        jnp.asarray(twiddle),
    )
    return next_row.reshape(green_row.shape), derivative.reshape(green_row.shape)


def solution(mesh):
    return jax.shard_map(
        local,
        mesh=mesh,
        in_specs=(
            P(None, None, None, "ta", "ka"),
            P(None, None, None, "ta", "ka"),
            P(None, None, None, "ta", "ka"),
            P(),
            P(None, None, None, "ta", None, "ka"),
            P(None, None, None, "ta", None, "ka"),
            P(),
            P(),
        ),
        out_specs=(P(None, None, None, "ta", "ka"), P(None, None, None, "ta", "ka")),
        check_vma=False,
    )
```

```python
import math

import jax
import jax.numpy as jnp
import numpy as np
from jax import lax
from jax.experimental import pallas as pl
from jax.experimental.pallas import tpu as pltpu
from jax.sharding import PartitionSpec as P

KS = 32
MESH = pl.DeviceIdType.MESH
F32 = jnp.float32
BF16 = jnp.bfloat16

time_step = 0.1
drive_amp = 1.0
drive_freq = 0.37


def split_np(x):
    hi = x.astype(np.float32).astype(jnp.bfloat16)
    lo = (x - hi.astype(np.float64)).astype(np.float32).astype(jnp.bfloat16)
    return hi, lo


def tables():
    ka, x1 = np.meshgrid(np.arange(8), np.arange(8), indexing="ij")
    c8, s8 = np.cos(2 * np.pi * ka * x1 / 8), np.sin(2 * np.pi * ka * x1 / 8)
    eye = np.eye(4)
    fwd = np.zeros((2, 8, 4, 8, 2, 4))
    bwd = np.zeros((8, 2, 4, 2, 8, 4))
    for k in range(8):
        for x in range(8):
            c, s = c8[k, x] * eye / KS, s8[k, x] * eye / KS
            fwd[0, x, :, k, 0, :] = c
            fwd[0, x, :, k, 1, :] = -s
            fwd[1, x, :, k, 0, :] = s
            fwd[1, x, :, k, 1, :] = c
            bwd[k, 0, :, 0, x, :] = c
            bwd[k, 0, :, 1, x, :] = s
            bwd[k, 1, :, 0, x, :] = -s
            bwd[k, 1, :, 1, x, :] = c
    left = []
    for m in (fwd.reshape(64, 64), bwd.reshape(64, 64)):
        hi, lo = split_np(m)
        left.append(np.concatenate([hi, lo, hi], axis=1))
    left = np.stack(left)
    lane = np.arange(128)
    j, y = lane // 32, lane % 32
    angle = 2 * np.pi * (np.outer(j, j) / 4 + np.outer(y, y) / 32)
    c, s = np.cos(angle), np.sin(angle)
    right = []
    for m in (np.block([[c, s], [-s, c]]), np.block([[c, -s], [s, c]])):
        right.extend(split_np(m))
    right = np.stack(right)
    row = np.arange(32) // 4
    tw = 2 * np.pi * np.outer(row, j) / 32
    twiddle = np.stack([np.cos(tw), np.sin(tw)]).astype(np.float32)
    return left, right, twiddle


def split(x):
    hi = x.astype(BF16)
    lo = (x - hi.astype(F32)).astype(BF16)
    return hi, lo


def mm(a, b):
    return jnp.dot(a, b, preferred_element_type=F32)


def left_product(table, x):
    hi, lo = split(x)
    return mm(table, jnp.concatenate([hi, hi, lo], axis=0))


def right_product(hi_table, lo_table, x):
    rows = x.shape[0]
    hi, lo = split(x)
    both = mm(jnp.concatenate([hi, lo], axis=0), hi_table)
    return both[:rows] + both[rows:] + mm(hi, lo_table)


def order(i):
    half = (i + 1) // 2
    return 4 + half - 2 * half * (i % 2)


def kernel(
    onsite_hbm, table_hbm, begin_hbm, green_hbm, less_hbm, ret_hbm, adv_hbm, les_hbm,
    left_hbm, right_hbm, twiddle_hbm,
    next_row, derivative,
    onsite, table, begin, green, less, ret, left, right, twiddle,
    raw, slab, oslab, isend, irecv, bsend, brecv, screens, ssend, srecv, sig,
    own, ysend, yrecv, zsend, zrecv, msend, mrecv, orecv, macc, gbuf, hg, first,
    in_sem, os_sem, or_sem, is_sem, ir_sem, gs_sem, gr_sem, ss_sem, sr_sem,
    ys_sem, yr_sem, zs_sem, zr_sem, ms_sem, mr_sem, oq_sem, ready,
):
    ta, ka = lax.axis_index("ta"), lax.axis_index("ka")
    z, y, core = ta // 4, (ta // 2) % 2, ta % 2
    sibling = ta + 1 - 2 * core
    across = ta + 2 - 4 * y

    loads = [
        pltpu.make_async_copy(src, dst, in_sem.at[i])
        for i, (src, dst) in enumerate(
            (
                (less_hbm, less), (ret_hbm, ret), (green_hbm, green), (table_hbm, table),
                (adv_hbm, raw.at[0]), (les_hbm, raw.at[1]), (onsite_hbm, onsite),
                (begin_hbm, begin), (left_hbm, left), (right_hbm, right), (twiddle_hbm, twiddle),
            )
        )
    ]
    for copy in loads:
        copy.start()

    barrier = pltpu.get_barrier_semaphore()
    for i in range(1, 8):
        pl.semaphore_signal(barrier, inc=1, device_id=(ta, (ka + i) % 8), device_id_type=MESH)
        pl.semaphore_signal(barrier, inc=1, device_id=(sibling, (ka + i) % 8), device_id_type=MESH)
        pl.semaphore_signal(barrier, inc=1, device_id=((ta + 4 * i) % 32, ka), device_id_type=MESH)
    pl.semaphore_signal(barrier, inc=1, device_id=(sibling, ka), device_id_type=MESH)
    pl.semaphore_signal(barrier, inc=1, device_id=(across, ka), device_id_type=MESH)

    for copy in loads[:4]:
        copy.wait()
    for n, ref in enumerate((less, ret, green)):
        for d in range(8):
            isend[d, 8 * n : 8 * n + 8, :] = ref[pl.ds(d, 8, stride=8), :]
    pl.semaphore_wait(barrier, 23)

    def describe(src, dst, ssem, rsem, to):
        return pltpu.make_async_remote_copy(
            src_ref=src, dst_ref=dst, send_sem=ssem, recv_sem=rsem,
            device_id=to, device_id_type=MESH,
        )

    def push(src, dst, ssem, rsem, to):
        describe(src, dst, ssem, rsem, to).start()

    def arrived(dst, rsem):
        describe(dst, dst, rsem, rsem, (sibling, ka)).wait_recv()

    def sent(src, ssem):
        describe(src, src, ssem, ssem, (sibling, ka)).wait_send()

    def exchange(src, dst, ssem, rsem):
        for i in range(7, 0, -1):
            peer = (ka + i) % 8
            push(src.at[peer], dst.at[ka], ssem.at[i], rsem.at[ka], (ta, peer))
        dst[ka] = src[ka]

    def collect(dst, rsem):
        for i in range(1, 8):
            peer = (ka + i) % 8
            arrived(dst.at[peer], rsem.at[peer])

    exchange(isend, irecv, is_sem, ir_sem)
    for i in range(1, 8):
        pl.semaphore_signal(ready, inc=1, device_id=((ta + 4 * i) % 32, ka), device_id_type=MESH)

    row = lax.broadcasted_iota(jnp.int32, (256, 1), 0)
    col = lax.broadcasted_iota(jnp.int32, (256, 256), 1)
    place = row // 8
    source = (
        ((row // 2) % 4) * 64 + (place % 8) * 8 + ((place // 8) % 2) * 4
        + ((core + place // 16) % 2) * 2 + row % 2
    )
    picked = source == col
    lane = lax.broadcasted_iota(jnp.int32, (1, 256), 1) % 64
    tau = jnp.zeros((1, 256), jnp.int32)
    for i in range(32):
        tau = jnp.where(lane // 2 == i, 2 * table[i], tau)
    tau = tau + lane % 2
    now = 2 * table[ta]
    plain = jnp.where(picked, 1.0, 0.0).astype(BF16)
    masked = [
        jnp.where(picked & (now + s <= tau), 1.0, 0.0).astype(BF16) for s in range(2)
    ]
    for copy in loads[4:]:
        copy.wait()

    def relay(b, carry):
        for kind in range(2):
            for s in range(2):
                parts = [
                    jnp.concatenate([raw[kind, q, b, c, s] for c in range(4)], axis=0)
                    for q in range(2)
                ]
                moved = mm(masked[s] if kind == 0 else plain, jnp.concatenate(parts, axis=1))
                re, im = moved[:, :128], moved[:, 128:]
                d = b * 2 + s
                slab[kind, 0, core * 8 + d] = re[:128].reshape(16, 8, 128)
                slab[kind, 1, core * 8 + d] = im[:128].reshape(16, 8, 128)
                slab[kind, 2, core * 8 + d] = (re[:128] + im[:128]).reshape(16, 8, 128)
                oslab[kind, 0, d] = re[128:].reshape(16, 8, 128)
                oslab[kind, 1, d] = im[128:].reshape(16, 8, 128)
        return carry

    lax.fori_loop(0, 4, relay, 0)
    for kind in range(2):
        for q in range(2):
            push(
                oslab.at[kind, q], slab.at[kind, q, pl.ds(core * 8, 8)],
                os_sem.at[kind, q], or_sem.at[kind, q], (sibling, ka),
            )

    shift = drive_amp * jnp.sin(
        jnp.full((64, 128), drive_freq, F32) * (begin[0] + 64).astype(F32)
    )
    k_lane = lax.broadcasted_iota(jnp.int32, (64, 128), 1)
    k_row = lax.broadcasted_iota(jnp.int32, (64, 128), 0)
    factor = 2.0 * math.pi / KS

    def dispersed(group, lane, by):
        return -2.0 * (
            jnp.cos((4 * group + lane // KS).astype(F32) * factor + by)
            + jnp.cos((lane % KS).astype(F32) * factor)
        )

    e_all = dispersed(k_row // 8, k_lane, shift)
    e = dispersed(ka, k_lane[:8], shift[:8])

    at_row = lax.broadcasted_iota(jnp.int32, (64, 64), 0)
    at_col = lax.broadcasted_iota(jnp.int32, (64, 64), 1)
    entry = jnp.where(at_row // 8 == at_col // 8, at_row % 8 * 8 + at_col % 8, -1)
    turn = jnp.zeros((64, 64), F32)
    for a in range(4):
        for b in range(4):
            o_re, o_im = onsite[0, a, b], onsite[1, a, b]
            turn = jnp.where(entry == 8 * a + b, o_re, turn)
            turn = jnp.where(entry == 8 * (a + 4) + b + 4, o_re, turn)
            turn = jnp.where(entry == 8 * a + b + 4, -o_im, turn)
            turn = jnp.where(entry == 8 * (a + 4) + b, o_im, turn)
    turn_hi, turn_lo = split(turn)
    turn = jnp.concatenate([turn_hi, turn_lo, turn_hi], axis=1)

    tw_c, tw_s = twiddle[0], twiddle[1]

    def to_space(tiles):
        mixed = left_product(left[0], tiles)
        n = tiles.shape[1] // 128
        turned = []
        for i in range(n):
            re, im = (mixed[32 * p : 32 * p + 32, 128 * i : 128 * i + 128] for p in range(2))
            turned.append(
                jnp.concatenate([re * tw_c - im * tw_s, re * tw_s + im * tw_c], axis=1)
            )
        out = right_product(right[0], right[1], jnp.concatenate(turned, axis=0))
        return [out[32 * i : 32 * i + 32] for i in range(n)]

    def to_momenta(fields):
        out = right_product(right[2], right[3], jnp.concatenate(fields, axis=0))
        turned = []
        for i in range(2):
            re, im = out[32 * i : 32 * i + 32, :128], out[32 * i : 32 * i + 32, 128:]
            turned.append(
                jnp.concatenate([re * tw_c + im * tw_s, im * tw_c - re * tw_s], axis=0)
            )
        return left_product(left[1], jnp.concatenate(turned, axis=1))

    collect(irecv, ir_sem)
    tiles = jnp.concatenate(
        [irecv[:, 8 * n : 8 * n + 8, :].reshape(64, 128) for n in range(3)], axis=1
    )
    w_less, w_ret, space = to_space(tiles)
    screens[0] = w_less
    screens[1] = w_ret

    def blocks(js):
        def terms(u, acc):
            kind, half = u // 2, u % 2
            acc = list(acc)
            for v in range(8):
                sd = half * 8 + v
                for q in range(3):
                    values = [slab[kind, q, sd, j] for j in js]
                    for a in range(4):
                        factor = sig[kind, q, sd, a]
                        for n in range(2):
                            at = (n * 4 + a) * 3 + q
                            acc[at] = acc[at] + factor * values[n]
            return tuple(acc)

        zero = jnp.zeros((8, 128), F32)
        flat = lax.fori_loop(0, 4, terms, (zero,) * 24)
        acc = [[flat[(n * 4 + a) * 3 : (n * 4 + a) * 3 + 3] for a in range(4)] for n in range(2)]
        out = []
        for n in range(2):
            re = [acc[n][a][0] - acc[n][a][1] for a in range(4)]
            im = [acc[n][a][2] - acc[n][a][0] - acc[n][a][1] for a in range(4)]
            out.append(re + im)
        return out

    def reduced(r):
        def to_across(piece, carry):
            places = [(z + order(2 * piece + n)) % 8 for n in range(2)]
            out = blocks([(1 - y) * 8 + p for p in places])
            for n in range(2):
                i = 2 * piece + n
                for m in range(8):
                    ysend[r, i, 8 * m : 8 * m + 8] = out[n][m]
                push(ysend.at[r, i], yrecv.at[r, i], ys_sem.at[r, i], yr_sem.at[r, i], (across, ka))
            return carry

        lax.fori_loop(0, 4, to_across, 0)

        def mine(piece, carry):
            places = [(z + order(2 * piece + n)) % 8 for n in range(2)]
            out = blocks([y * 8 + p for p in places])
            for n in range(2):
                for m in range(8):
                    own[2 * piece + n, 8 * m : 8 * m + 8] = out[n][m]
            return carry

        lax.fori_loop(0, 4, mine, 0)

    def to_owner():
        for i in range(8):
            arrived(yrecv.at[2, i], yr_sem.at[2, i])
            if i < 7:
                zsend[i] = own[i] + yrecv[2, i]
                away = (z + order(i)) % 8
                push(
                    zsend.at[i], zrecv.at[z], zs_sem.at[i], zr_sem.at[z],
                    (away * 4 + ta % 4, ka),
                )
        total = own[7] + yrecv[2, 7] + hg[...]
        for i in range(7):
            peer = (z + order(i)) % 8
            arrived(zrecv.at[peer], zr_sem.at[peer])
            total = total + zrecv[peer]
        return total

    def to_fields(r):
        def tiles_of(i):
            arrived(yrecv.at[r, i], yr_sem.at[r, i])
            zsend[i] = own[i] + yrecv[r, i]
            for d in range(8):
                msend[r, i, d] = zsend[i, pl.ds(d, 8, stride=8), :]

        def away_block(i, carry):
            tiles_of(i)
            away = ((z + order(i)) % 8) * 4 + ta % 4
            for n in range(8):
                peer = (ka + 6 + n) % 8
                push(
                    msend.at[r, i, peer], mrecv.at[r, z * 8 + ka], ms_sem.at[r, i],
                    mr_sem.at[r, z], (away, peer),
                )
            return carry

        lax.fori_loop(0, 7, away_block, 0)
        tiles_of(7)
        for n in range(1, 8):
            i = (n + 4) % 7 + 1
            peer = (ka + i) % 8
            push(
                msend.at[r, 7, peer], orecv.at[r, i - 1], ms_sem.at[r, 7], oq_sem.at[r],
                (ta, peer),
            )
        total = hg[...]
        for i in range(7):
            group = pl.ds(((z + order(i)) % 8) * 8, 8)
            arrived(mrecv.at[r, group], mr_sem.at[r, (z + order(i)) % 8])
            total = total + mrecv[r, group].reshape(64, 128)
        macc[...] = total.reshape(8, 8, 128)
        macc[ka] += msend[r, 7, ka]
        arrived(orecv.at[r], oq_sem.at[r])
        for i in range(1, 8):
            macc[(ka + 8 - i) % 8] += orecv[r, i - 1]
        total = macc[...]
        return jnp.concatenate([total[:, 4:], -total[:, :4]], axis=1).reshape(64, 128)

    green_all = irecv[:, 16:24, :].reshape(64, 128)
    state = green_all
    for r in range(3):
        if r > 0:
            (space,) = to_space(state)
        re, im = space[:, :128], space[:, 128:]
        fields = []
        for kind in range(2):
            w_re, w_im = screens[kind, :, :128], screens[kind, :, 128:]
            fields.append(
                jnp.concatenate([-(re * w_im + im * w_re), re * w_re - im * w_im], axis=1)
            )
        sigma = to_momenta(fields)
        for kind in range(2):
            ssend[r, :, kind] = sigma[:, 128 * kind : 128 * kind + 128].reshape(8, 8, 128)
        slot = core * 8 + ka
        for i in range(7, 0, -1):
            peer = (ka + i) % 8
            for n, to in enumerate((ta, sibling)):
                push(
                    ssend.at[r, peer], srecv.at[r, slot], ss_sem.at[r, 2 * i + n],
                    sr_sem.at[r, slot], (to, peer),
                )
        push(
            ssend.at[r, ka], srecv.at[r, slot], ss_sem.at[r, 0], sr_sem.at[r, slot], (sibling, ka)
        )
        srecv[r, slot] = ssend[r, ka]

        if r < 2:
            hg[...] = left_product(turn, state) + e_all * state
        else:
            for d in range(8):
                bsend[d, :8] = state[8 * d : 8 * d + 8]
                bsend[d, 8:] = first[8 * d : 8 * d + 8]
            exchange(bsend, brecv, gs_sem, gr_sem)

        if r == 0:
            for kind in range(2):
                for q in range(2):
                    theirs = slab.at[kind, q, pl.ds((1 - core) * 8, 8)]
                    arrived(theirs, or_sem.at[kind, q])
                for d in range(8):
                    sd = (1 - core) * 8 + d
                    slab[kind, 2, sd] = slab[kind, 0, sd] + slab[kind, 1, sd]

        for i in range(8):
            peer = (ka + i) % 8
            for n in range(2):
                if i + n > 0:
                    sd = ((core + n) % 2) * 8 + peer
                    arrived(srecv.at[r, sd], sr_sem.at[r, sd])
        for sd in range(16):
            for kind in range(2):
                tile = srecv[r, sd, kind].astype(BF16).astype(F32)
                for a in range(4):
                    s_re = jnp.broadcast_to(tile[a : a + 1], (8, 128))
                    s_im = jnp.broadcast_to(tile[4 + a : 5 + a], (8, 128))
                    sig[kind, 0, sd, a] = s_re
                    sig[kind, 1, sd, a] = s_im
                    sig[kind, 2, sd, a] = s_re + s_im

        if r == 0:
            pl.semaphore_wait(ready, 7)
        reduced(r)
        if r < 2:
            rate = to_fields(r)
            if r == 0:
                first[...] = rate
                state = green_all + time_step * rate
            else:
                state = green_all + (0.5 * time_step) * (first[...] + rate)
            continue

        collect(brecv, gr_sem)
        for d in range(8):
            gbuf[pl.ds(d, 8, stride=8), :] = brecv[d, :8]
            first[pl.ds(d, 8, stride=8), :] = brecv[d, 8:]
        rows = [gbuf[8 * m : 8 * m + 8] for m in range(8)]
        for a in range(4):
            re, im = e * rows[a], e * rows[4 + a]
            for b in range(4):
                o_re, o_im = onsite[0, a, b], onsite[1, a, b]
                re = re + o_re * rows[b] - o_im * rows[4 + b]
                im = im + o_re * rows[4 + b] + o_im * rows[b]
            hg[8 * a : 8 * a + 8] = re
            hg[32 + 8 * a : 40 + 8 * a] = im
        total = to_owner()
        rate = jnp.concatenate([total[32:], -total[:32]], axis=0)
        next_row[...] = green[...] + (0.5 * time_step) * (first[...] + rate)
        derivative[...] = rate

    for kind in range(2):
        for q in range(2):
            sent(oslab.at[kind, q], os_sem.at[kind, q])
    for i in range(1, 8):
        sent(isend.at[(ka + i) % 8], is_sem.at[i])
        sent(bsend.at[(ka + i) % 8], gs_sem.at[i])
        sent(zsend.at[i - 1], zs_sem.at[i - 1])
    for r in range(3):
        for i in range(1, 8):
            for n in range(2):
                sent(ssend.at[r, (ka + i) % 8], ss_sem.at[r, 2 * i + n])
        sent(ssend.at[r, ka], ss_sem.at[r, 0])
        for i in range(8):
            sent(ysend.at[r, i], ys_sem.at[r, i])
        if r < 2:
            for i in range(7):
                sent(msend.at[r, i], ms_sem.at[r, i])
            sent(msend.at[r, 7, pl.ds(0, 7)], ms_sem.at[r, 7])


def local(
    green_row, screen_lesser, screen_retarded, onsite, lesser_slab, advanced_slab, slab_start,
    block_table,
):
    left, right, twiddle = tables()

    def hbm():
        return pl.BlockSpec(memory_space=pltpu.HBM)

    def vmem():
        return pl.BlockSpec(memory_space=pltpu.VMEM)

    def scratch(*dims, kind=F32):
        return pltpu.VMEM(dims, kind)

    def sems(*dims):
        return pltpu.SemaphoreType.DMA(dims)

    rows = jax.ShapeDtypeStruct((64, 128), F32)
    next_row, derivative = pl.pallas_call(
        kernel,
        name="gw_step",
        out_shape=(rows, rows),
        in_specs=[hbm()] * 11,
        out_specs=(vmem(), vmem()),
        scratch_shapes=[
            pltpu.SMEM((2, 4, 4), F32),
            pltpu.SMEM((32,), jnp.int32),
            pltpu.SMEM((1,), jnp.int32),
            scratch(64, 128),
            scratch(64, 128),
            scratch(64, 128),
            scratch(2, 64, 192, kind=BF16),
            scratch(4, 256, 256, kind=BF16),
            scratch(2, 32, 128),
            scratch(2, 2, 4, 4, 2, 64, 128, kind=BF16),
            scratch(2, 3, 16, 16, 8, 128),
            scratch(2, 2, 8, 16, 8, 128),
            scratch(8, 24, 128),
            scratch(8, 24, 128),
            scratch(8, 16, 128),
            scratch(8, 16, 128),
            scratch(2, 32, 256),
            scratch(3, 8, 2, 8, 128),
            scratch(3, 16, 2, 8, 128),
            scratch(2, 3, 16, 4, 8, 128),
            scratch(8, 64, 128),
            scratch(3, 8, 64, 128),
            scratch(3, 8, 64, 128),
            scratch(8, 64, 128),
            scratch(8, 64, 128),
            scratch(2, 8, 8, 8, 128),
            scratch(2, 64, 8, 128),
            scratch(2, 7, 8, 128),
            scratch(8, 8, 128),
            scratch(64, 128),
            scratch(64, 128),
            scratch(64, 128),
            sems(11),
            sems(2, 2), sems(2, 2),
            sems(8), sems(8),
            sems(8), sems(8),
            sems(3, 16), sems(3, 16),
            sems(3, 8), sems(3, 8),
            sems(7), sems(8),
            sems(2, 8), sems(2, 8), sems(2),
            pltpu.SemaphoreType.REGULAR,
        ],
        compiler_params=pltpu.CompilerParams(
            collective_id=0, has_side_effects=True, vmem_limit_bytes=56 * 2**20
        ),
    )(
        onsite,
        block_table,
        slab_start,
        green_row.reshape(64, 128),
        screen_lesser.reshape(64, 128),
        screen_retarded.reshape(64, 128),
        advanced_slab,
        lesser_slab,
        jnp.asarray(left),
        jnp.asarray(right),
        jnp.asarray(twiddle),
    )
    return next_row.reshape(green_row.shape), derivative.reshape(green_row.shape)


def solution(mesh):
    return jax.shard_map(
        local,
        mesh=mesh,
        in_specs=(
            P(None, None, None, "ta", "ka"),
            P(None, None, None, "ta", "ka"),
            P(None, None, None, "ta", "ka"),
            P(),
            P(None, None, None, "ta", None, "ka"),
            P(None, None, None, "ta", None, "ka"),
            P(),
            P(),
        ),
        out_specs=(P(None, None, None, "ta", "ka"), P(None, None, None, "ta", "ka")),
        check_vma=False,
    )
```

```python
import math

import jax
import jax.numpy as jnp
import numpy as np
from jax import lax
from jax.experimental import pallas as pl
from jax.experimental.pallas import tpu as pltpu
from jax.sharding import PartitionSpec as P

KS = 32
MESH = pl.DeviceIdType.MESH
F32 = jnp.float32
BF16 = jnp.bfloat16

time_step = 0.1
drive_amp = 1.0
drive_freq = 0.37


def split_np(x):
    hi = x.astype(np.float32).astype(jnp.bfloat16)
    lo = (x - hi.astype(np.float64)).astype(np.float32).astype(jnp.bfloat16)
    return hi, lo


def tables():
    ka, x1 = np.meshgrid(np.arange(8), np.arange(8), indexing="ij")
    c8, s8 = np.cos(2 * np.pi * ka * x1 / 8), np.sin(2 * np.pi * ka * x1 / 8)
    eye = np.eye(4)
    fwd = np.zeros((2, 8, 4, 8, 2, 4))
    bwd = np.zeros((8, 2, 4, 2, 8, 4))
    for k in range(8):
        for x in range(8):
            c, s = c8[k, x] * eye / KS, s8[k, x] * eye / KS
            fwd[0, x, :, k, 0, :] = c
            fwd[0, x, :, k, 1, :] = -s
            fwd[1, x, :, k, 0, :] = s
            fwd[1, x, :, k, 1, :] = c
            bwd[k, 0, :, 0, x, :] = c
            bwd[k, 0, :, 1, x, :] = s
            bwd[k, 1, :, 0, x, :] = -s
            bwd[k, 1, :, 1, x, :] = c
    left = []
    for m in (fwd.reshape(64, 64), bwd.reshape(64, 64)):
        hi, lo = split_np(m)
        left.append(np.concatenate([hi, lo, hi], axis=1))
    left = np.stack(left)
    lane = np.arange(128)
    j, y = lane // 32, lane % 32
    angle = 2 * np.pi * (np.outer(j, j) / 4 + np.outer(y, y) / 32)
    c, s = np.cos(angle), np.sin(angle)
    right = []
    for m in (np.block([[c, s], [-s, c]]), np.block([[c, -s], [s, c]])):
        right.extend(split_np(m))
    right = np.stack(right)
    row = np.arange(32) // 4
    tw = 2 * np.pi * np.outer(row, j) / 32
    twiddle = np.stack([np.cos(tw), np.sin(tw)]).astype(np.float32)
    return left, right, twiddle


def split(x):
    hi = x.astype(BF16)
    lo = (x - hi.astype(F32)).astype(BF16)
    return hi, lo


def mm(a, b):
    return jnp.dot(a, b, preferred_element_type=F32)


def left_product(table, x):
    hi, lo = split(x)
    return mm(table, jnp.concatenate([hi, hi, lo], axis=0))


def right_product(hi_table, lo_table, x):
    rows = x.shape[0]
    hi, lo = split(x)
    both = mm(jnp.concatenate([hi, lo], axis=0), hi_table)
    return both[:rows] + both[rows:] + mm(hi, lo_table)


def order(i):
    half = (i + 1) // 2
    return 4 + half - 2 * half * (i % 2)


def kernel(
    onsite_hbm, table_hbm, begin_hbm, green_hbm, less_hbm, ret_hbm, adv_hbm, les_hbm,
    left_hbm, right_hbm, twiddle_hbm,
    next_row, derivative,
    onsite, table, begin, green, less, ret, left, right, twiddle,
    raw, slab, oslab, isend, irecv, bsend, brecv, screens, ssend, srecv, sig,
    own, ysend, yrecv, zsend, zrecv, msend, mrecv, orecv, macc, gbuf, hg, first,
    in_sem, os_sem, or_sem, is_sem, ir_sem, gs_sem, gr_sem, ss_sem, sr_sem,
    ys_sem, yr_sem, zs_sem, zr_sem, ms_sem, mr_sem, oq_sem, ready,
):
    ta, ka = lax.axis_index("ta"), lax.axis_index("ka")
    z, y, core = ta // 4, (ta // 2) % 2, ta % 2
    sibling = ta + 1 - 2 * core
    across = ta + 2 - 4 * y

    loads = [
        pltpu.make_async_copy(src, dst, in_sem.at[i])
        for i, (src, dst) in enumerate(
            (
                (less_hbm, less), (ret_hbm, ret), (green_hbm, green), (table_hbm, table),
                (adv_hbm, raw.at[0]), (les_hbm, raw.at[1]), (onsite_hbm, onsite),
                (begin_hbm, begin), (left_hbm, left), (right_hbm, right), (twiddle_hbm, twiddle),
            )
        )
    ]
    for copy in loads:
        copy.start()

    barrier = pltpu.get_barrier_semaphore()
    for i in range(1, 8):
        pl.semaphore_signal(barrier, inc=1, device_id=(ta, (ka + i) % 8), device_id_type=MESH)
        pl.semaphore_signal(barrier, inc=1, device_id=(sibling, (ka + i) % 8), device_id_type=MESH)
        pl.semaphore_signal(barrier, inc=1, device_id=((ta + 4 * i) % 32, ka), device_id_type=MESH)
    pl.semaphore_signal(barrier, inc=1, device_id=(sibling, ka), device_id_type=MESH)
    pl.semaphore_signal(barrier, inc=1, device_id=(across, ka), device_id_type=MESH)

    for copy in loads[:4]:
        copy.wait()
    for n, ref in enumerate((less, ret, green)):
        for d in range(8):
            isend[d, 8 * n : 8 * n + 8, :] = ref[pl.ds(d, 8, stride=8), :]
    pl.semaphore_wait(barrier, 23)

    def describe(src, dst, ssem, rsem, to):
        return pltpu.make_async_remote_copy(
            src_ref=src, dst_ref=dst, send_sem=ssem, recv_sem=rsem,
            device_id=to, device_id_type=MESH,
        )

    def push(src, dst, ssem, rsem, to):
        describe(src, dst, ssem, rsem, to).start()

    def arrived(dst, rsem):
        describe(dst, dst, rsem, rsem, (sibling, ka)).wait_recv()

    def sent(src, ssem):
        describe(src, src, ssem, ssem, (sibling, ka)).wait_send()

    def exchange(src, dst, ssem, rsem):
        for i in range(7, 0, -1):
            peer = (ka + i) % 8
            push(src.at[peer], dst.at[ka], ssem.at[i], rsem.at[ka], (ta, peer))
        dst[ka] = src[ka]

    def collect(dst, rsem):
        for i in range(1, 8):
            peer = (ka + i) % 8
            arrived(dst.at[peer], rsem.at[peer])

    exchange(isend, irecv, is_sem, ir_sem)
    for i in range(1, 8):
        pl.semaphore_signal(ready, inc=1, device_id=((ta + 4 * i) % 32, ka), device_id_type=MESH)

    row = lax.broadcasted_iota(jnp.int32, (256, 1), 0)
    col = lax.broadcasted_iota(jnp.int32, (256, 256), 1)
    place = row // 8
    source = (
        ((row // 2) % 4) * 64 + (place % 8) * 8 + ((place // 8) % 2) * 4
        + ((core + place // 16) % 2) * 2 + row % 2
    )
    picked = source == col
    lane = lax.broadcasted_iota(jnp.int32, (1, 256), 1) % 64
    tau = jnp.zeros((1, 256), jnp.int32)
    for i in range(32):
        tau = jnp.where(lane // 2 == i, 2 * table[i], tau)
    tau = tau + lane % 2
    now = 2 * table[ta]
    plain = jnp.where(picked, 1.0, 0.0).astype(BF16)
    masked = [
        jnp.where(picked & (now + s <= tau), 1.0, 0.0).astype(BF16) for s in range(2)
    ]
    for copy in loads[4:]:
        copy.wait()

    def relay(b, carry):
        for kind in range(2):
            for s in range(2):
                parts = [
                    jnp.concatenate([raw[kind, q, b, c, s] for c in range(4)], axis=0)
                    for q in range(2)
                ]
                moved = mm(masked[s] if kind == 0 else plain, jnp.concatenate(parts, axis=1))
                re, im = moved[:, :128], moved[:, 128:]
                d = b * 2 + s
                slab[kind, 0, core * 8 + d] = re[:128].reshape(16, 8, 128)
                slab[kind, 1, core * 8 + d] = im[:128].reshape(16, 8, 128)
                slab[kind, 2, core * 8 + d] = (re[:128] + im[:128]).reshape(16, 8, 128)
                oslab[kind, 0, d] = re[128:].reshape(16, 8, 128)
                oslab[kind, 1, d] = im[128:].reshape(16, 8, 128)
        return carry

    lax.fori_loop(0, 4, relay, 0)
    for kind in range(2):
        for q in range(2):
            push(
                oslab.at[kind, q], slab.at[kind, q, pl.ds(core * 8, 8)],
                os_sem.at[kind, q], or_sem.at[kind, q], (sibling, ka),
            )

    shift = drive_amp * jnp.sin(
        jnp.full((64, 128), drive_freq, F32) * (begin[0] + 64).astype(F32)
    )
    k_lane = lax.broadcasted_iota(jnp.int32, (64, 128), 1)
    k_row = lax.broadcasted_iota(jnp.int32, (64, 128), 0)
    factor = 2.0 * math.pi / KS

    def dispersed(group, lane, by):
        return -2.0 * (
            jnp.cos((4 * group + lane // KS).astype(F32) * factor + by)
            + jnp.cos((lane % KS).astype(F32) * factor)
        )

    e_all = dispersed(k_row // 8, k_lane, shift)
    e = dispersed(ka, k_lane[:8], shift[:8])

    at_row = lax.broadcasted_iota(jnp.int32, (64, 64), 0)
    at_col = lax.broadcasted_iota(jnp.int32, (64, 64), 1)
    entry = jnp.where(at_row // 8 == at_col // 8, at_row % 8 * 8 + at_col % 8, -1)
    turn = jnp.zeros((64, 64), F32)
    for a in range(4):
        for b in range(4):
            o_re, o_im = onsite[0, a, b], onsite[1, a, b]
            turn = jnp.where(entry == 8 * a + b, o_re, turn)
            turn = jnp.where(entry == 8 * (a + 4) + b + 4, o_re, turn)
            turn = jnp.where(entry == 8 * a + b + 4, -o_im, turn)
            turn = jnp.where(entry == 8 * (a + 4) + b, o_im, turn)
    turn_hi, turn_lo = split(turn)
    turn = jnp.concatenate([turn_hi, turn_lo, turn_hi], axis=1)

    tw_c, tw_s = twiddle[0], twiddle[1]

    def to_space(tiles):
        mixed = left_product(left[0], tiles)
        n = tiles.shape[1] // 128
        turned = []
        for i in range(n):
            re, im = (mixed[32 * p : 32 * p + 32, 128 * i : 128 * i + 128] for p in range(2))
            turned.append(
                jnp.concatenate([re * tw_c - im * tw_s, re * tw_s + im * tw_c], axis=1)
            )
        out = right_product(right[0], right[1], jnp.concatenate(turned, axis=0))
        return [out[32 * i : 32 * i + 32] for i in range(n)]

    def to_momenta(fields):
        out = right_product(right[2], right[3], jnp.concatenate(fields, axis=0))
        turned = []
        for i in range(2):
            re, im = out[32 * i : 32 * i + 32, :128], out[32 * i : 32 * i + 32, 128:]
            turned.append(
                jnp.concatenate([re * tw_c + im * tw_s, im * tw_c - re * tw_s], axis=0)
            )
        return left_product(left[1], jnp.concatenate(turned, axis=1))

    collect(irecv, ir_sem)
    tiles = jnp.concatenate(
        [irecv[:, 8 * n : 8 * n + 8, :].reshape(64, 128) for n in range(3)], axis=1
    )
    w_less, w_ret, space = to_space(tiles)
    screens[0] = w_less
    screens[1] = w_ret

    def blocks(js):
        def terms(u, acc):
            kind, half = u // 2, u % 2
            acc = list(acc)
            for v in range(8):
                sd = half * 8 + v
                for q in range(3):
                    values = [slab[kind, q, sd, j] for j in js]
                    for a in range(4):
                        factor = sig[kind, q, sd, a]
                        for n in range(2):
                            at = (n * 4 + a) * 3 + q
                            acc[at] = acc[at] + factor * values[n]
            return tuple(acc)

        zero = jnp.zeros((8, 128), F32)
        flat = lax.fori_loop(0, 4, terms, (zero,) * 24)
        acc = [[flat[(n * 4 + a) * 3 : (n * 4 + a) * 3 + 3] for a in range(4)] for n in range(2)]
        out = []
        for n in range(2):
            re = [acc[n][a][0] - acc[n][a][1] for a in range(4)]
            im = [acc[n][a][2] - acc[n][a][0] - acc[n][a][1] for a in range(4)]
            out.append(re + im)
        return out

    def reduced(r):
        def to_across(piece, carry):
            places = [(z + order(2 * piece + n)) % 8 for n in range(2)]
            out = blocks([(1 - y) * 8 + p for p in places])
            for n in range(2):
                i = 2 * piece + n
                for m in range(8):
                    ysend[r, i, 8 * m : 8 * m + 8] = out[n][m]
                push(ysend.at[r, i], yrecv.at[r, i], ys_sem.at[r, i], yr_sem.at[r, i], (across, ka))
            return carry

        lax.fori_loop(0, 4, to_across, 0)

        def mine(piece, carry):
            places = [(z + order(2 * piece + n)) % 8 for n in range(2)]
            out = blocks([y * 8 + p for p in places])
            for n in range(2):
                for m in range(8):
                    own[2 * piece + n, 8 * m : 8 * m + 8] = out[n][m]
            return carry

        lax.fori_loop(0, 4, mine, 0)

    def to_owner():
        for i in range(8):
            arrived(yrecv.at[2, i], yr_sem.at[2, i])
            if i < 7:
                zsend[i] = own[i] + yrecv[2, i]
                away = (z + order(i)) % 8
                push(
                    zsend.at[i], zrecv.at[z], zs_sem.at[i], zr_sem.at[z],
                    (away * 4 + ta % 4, ka),
                )
        total = own[7] + yrecv[2, 7] + hg[...]
        for i in range(7):
            peer = (z + order(i)) % 8
            arrived(zrecv.at[peer], zr_sem.at[peer])
            total = total + zrecv[peer]
        return total

    def to_fields(r):
        def tiles_of(i):
            arrived(yrecv.at[r, i], yr_sem.at[r, i])
            zsend[i] = own[i] + yrecv[r, i]
            for d in range(8):
                msend[r, i, d] = zsend[i, pl.ds(d, 8, stride=8), :]

        def away_block(i, carry):
            tiles_of(i)
            away = ((z + order(i)) % 8) * 4 + ta % 4
            for n in range(8):
                peer = (ka + 6 + n) % 8
                push(
                    msend.at[r, i, peer], mrecv.at[r, z * 8 + ka], ms_sem.at[r, i],
                    mr_sem.at[r, z], (away, peer),
                )
            return carry

        lax.fori_loop(0, 7, away_block, 0)
        tiles_of(7)
        for n in range(1, 8):
            i = (n + 4) % 7 + 1
            peer = (ka + i) % 8
            push(
                msend.at[r, 7, peer], orecv.at[r, i - 1], ms_sem.at[r, 7], oq_sem.at[r],
                (ta, peer),
            )
        total = hg[...]
        for i in range(7):
            group = pl.ds(((z + order(i)) % 8) * 8, 8)
            arrived(mrecv.at[r, group], mr_sem.at[r, (z + order(i)) % 8])
            total = total + mrecv[r, group].reshape(64, 128)
        macc[...] = total.reshape(8, 8, 128)
        macc[ka] += msend[r, 7, ka]
        arrived(orecv.at[r], oq_sem.at[r])
        for i in range(1, 8):
            macc[(ka + 8 - i) % 8] += orecv[r, i - 1]
        total = macc[...]
        return jnp.concatenate([total[:, 4:], -total[:, :4]], axis=1).reshape(64, 128)

    green_all = irecv[:, 16:24, :].reshape(64, 128)
    state = green_all
    for r in range(3):
        if r > 0:
            (space,) = to_space(state)
        re, im = space[:, :128], space[:, 128:]
        fields = []
        for kind in range(2):
            w_re, w_im = screens[kind, :, :128], screens[kind, :, 128:]
            fields.append(
                jnp.concatenate([-(re * w_im + im * w_re), re * w_re - im * w_im], axis=1)
            )
        sigma = to_momenta(fields)
        for kind in range(2):
            ssend[r, :, kind] = sigma[:, 128 * kind : 128 * kind + 128].reshape(8, 8, 128)
        slot = core * 8 + ka
        for i in range(7, 0, -1):
            peer = (ka + i) % 8
            for n, to in enumerate((ta, sibling)):
                push(
                    ssend.at[r, peer], srecv.at[r, slot], ss_sem.at[r, 2 * i + n],
                    sr_sem.at[r, slot], (to, peer),
                )
        push(
            ssend.at[r, ka], srecv.at[r, slot], ss_sem.at[r, 0], sr_sem.at[r, slot], (sibling, ka)
        )
        srecv[r, slot] = ssend[r, ka]

        if r < 2:
            hg[...] = left_product(turn, state) + e_all * state
        else:
            for d in range(8):
                bsend[d, :8] = state[8 * d : 8 * d + 8]
                bsend[d, 8:] = first[8 * d : 8 * d + 8]
            exchange(bsend, brecv, gs_sem, gr_sem)

        if r == 0:
            for kind in range(2):
                for q in range(2):
                    theirs = slab.at[kind, q, pl.ds((1 - core) * 8, 8)]
                    arrived(theirs, or_sem.at[kind, q])
                for d in range(8):
                    sd = (1 - core) * 8 + d
                    slab[kind, 2, sd] = slab[kind, 0, sd] + slab[kind, 1, sd]

        for i in range(8):
            peer = (ka + i) % 8
            for n in range(2):
                if i + n > 0:
                    sd = ((core + n) % 2) * 8 + peer
                    arrived(srecv.at[r, sd], sr_sem.at[r, sd])
        for sd in range(16):
            for kind in range(2):
                tile = srecv[r, sd, kind].astype(BF16).astype(F32)
                for a in range(4):
                    s_re = jnp.broadcast_to(tile[a : a + 1], (8, 128))
                    s_im = jnp.broadcast_to(tile[4 + a : 5 + a], (8, 128))
                    sig[kind, 0, sd, a] = s_re
                    sig[kind, 1, sd, a] = s_im
                    sig[kind, 2, sd, a] = s_re + s_im

        if r == 0:
            pl.semaphore_wait(ready, 7)
        reduced(r)
        if r < 2:
            rate = to_fields(r)
            if r == 0:
                first[...] = rate
                state = green_all + time_step * rate
            else:
                state = green_all + (0.5 * time_step) * (first[...] + rate)
            continue

        collect(brecv, gr_sem)
        for d in range(8):
            gbuf[pl.ds(d, 8, stride=8), :] = brecv[d, :8]
            first[pl.ds(d, 8, stride=8), :] = brecv[d, 8:]
        rows = [gbuf[8 * m : 8 * m + 8] for m in range(8)]
        for a in range(4):
            re, im = e * rows[a], e * rows[4 + a]
            for b in range(4):
                o_re, o_im = onsite[0, a, b], onsite[1, a, b]
                re = re + o_re * rows[b] - o_im * rows[4 + b]
                im = im + o_re * rows[4 + b] + o_im * rows[b]
            hg[8 * a : 8 * a + 8] = re
            hg[32 + 8 * a : 40 + 8 * a] = im
        total = to_owner()
        rate = jnp.concatenate([total[32:], -total[:32]], axis=0)
        next_row[...] = green[...] + (0.5 * time_step) * (first[...] + rate)
        derivative[...] = rate

    for kind in range(2):
        for q in range(2):
            sent(oslab.at[kind, q], os_sem.at[kind, q])
    for i in range(1, 8):
        sent(isend.at[(ka + i) % 8], is_sem.at[i])
        sent(bsend.at[(ka + i) % 8], gs_sem.at[i])
        sent(zsend.at[i - 1], zs_sem.at[i - 1])
    for r in range(3):
        for i in range(1, 8):
            for n in range(2):
                sent(ssend.at[r, (ka + i) % 8], ss_sem.at[r, 2 * i + n])
        sent(ssend.at[r, ka], ss_sem.at[r, 0])
        for i in range(8):
            sent(ysend.at[r, i], ys_sem.at[r, i])
        if r < 2:
            for i in range(7):
                sent(msend.at[r, i], ms_sem.at[r, i])
            sent(msend.at[r, 7, pl.ds(0, 7)], ms_sem.at[r, 7])


def local(
    green_row, screen_lesser, screen_retarded, onsite, lesser_slab, advanced_slab, slab_start,
    block_table,
):
    left, right, twiddle = tables()

    def hbm():
        return pl.BlockSpec(memory_space=pltpu.HBM)

    def vmem():
        return pl.BlockSpec(memory_space=pltpu.VMEM)

    def scratch(*dims, kind=F32):
        return pltpu.VMEM(dims, kind)

    def sems(*dims):
        return pltpu.SemaphoreType.DMA(dims)

    rows = jax.ShapeDtypeStruct((64, 128), F32)
    next_row, derivative = pl.pallas_call(
        kernel,
        name="gw_step",
        out_shape=(pltpu.VMEM((64, 128), F32), pltpu.VMEM((64, 128), F32)),
        in_specs=[hbm()] * 11,
        out_specs=(vmem(), vmem()),
        scratch_shapes=[
            pltpu.SMEM((2, 4, 4), F32),
            pltpu.SMEM((32,), jnp.int32),
            pltpu.SMEM((1,), jnp.int32),
            scratch(64, 128),
            scratch(64, 128),
            scratch(64, 128),
            scratch(2, 64, 192, kind=BF16),
            scratch(4, 256, 256, kind=BF16),
            scratch(2, 32, 128),
            scratch(2, 2, 4, 4, 2, 64, 128, kind=BF16),
            scratch(2, 3, 16, 16, 8, 128),
            scratch(2, 2, 8, 16, 8, 128),
            scratch(8, 24, 128),
            scratch(8, 24, 128),
            scratch(8, 16, 128),
            scratch(8, 16, 128),
            scratch(2, 32, 256),
            scratch(3, 8, 2, 8, 128),
            scratch(3, 16, 2, 8, 128),
            scratch(2, 3, 16, 4, 8, 128),
            scratch(8, 64, 128),
            scratch(3, 8, 64, 128),
            scratch(3, 8, 64, 128),
            scratch(8, 64, 128),
            scratch(8, 64, 128),
            scratch(2, 8, 8, 8, 128),
            scratch(2, 64, 8, 128),
            scratch(2, 7, 8, 128),
            scratch(8, 8, 128),
            scratch(64, 128),
            scratch(64, 128),
            scratch(64, 128),
            sems(11),
            sems(2, 2), sems(2, 2),
            sems(8), sems(8),
            sems(8), sems(8),
            sems(3, 16), sems(3, 16),
            sems(3, 8), sems(3, 8),
            sems(7), sems(8),
            sems(2, 8), sems(2, 8), sems(2),
            pltpu.SemaphoreType.REGULAR,
        ],
        compiler_params=pltpu.CompilerParams(
            collective_id=0, has_side_effects=True, vmem_limit_bytes=56 * 2**20
        ),
    )(
        onsite,
        block_table,
        slab_start,
        green_row.reshape(64, 128),
        screen_lesser.reshape(64, 128),
        screen_retarded.reshape(64, 128),
        advanced_slab,
        lesser_slab,
        jnp.asarray(left),
        jnp.asarray(right),
        jnp.asarray(twiddle),
    )
    return next_row.reshape(green_row.shape), derivative.reshape(green_row.shape)


def solution(mesh):
    return jax.shard_map(
        local,
        mesh=mesh,
        in_specs=(
            P(None, None, None, "ta", "ka"),
            P(None, None, None, "ta", "ka"),
            P(None, None, None, "ta", "ka"),
            P(),
            P(None, None, None, "ta", None, "ka"),
            P(None, None, None, "ta", None, "ka"),
            P(),
            P(),
        ),
        out_specs=(P(None, None, None, "ta", "ka"), P(None, None, None, "ta", "ka")),
        check_vma=False,
    )
```

```python
import math

import jax
import jax.numpy as jnp
import numpy as np
from jax import lax
from jax.experimental import pallas as pl
from jax.experimental.pallas import tpu as pltpu
from jax.sharding import PartitionSpec as P

KS = 32
PEERS = ((1, 2), (1, 1), (1, 3), (1, 0), (0, 2), (0, 1), (0, 3), (0, 0))
MESH = pl.DeviceIdType.MESH
F32 = jnp.float32
BF16 = jnp.bfloat16

time_step = 0.1
drive_amp = 1.0
drive_freq = 0.37


def split_np(x):
    hi = x.astype(np.float32).astype(jnp.bfloat16)
    lo = (x - hi.astype(np.float64)).astype(np.float32).astype(jnp.bfloat16)
    return hi, lo


def tables():
    ka, x1 = np.meshgrid(np.arange(8), np.arange(8), indexing="ij")
    c8, s8 = np.cos(2 * np.pi * ka * x1 / 8), np.sin(2 * np.pi * ka * x1 / 8)
    eye = np.eye(4)
    fwd = np.zeros((2, 8, 4, 8, 2, 4))
    bwd = np.zeros((8, 2, 4, 2, 8, 4))
    for k in range(8):
        for x in range(8):
            c, s = c8[k, x] * eye / KS, s8[k, x] * eye / KS
            fwd[0, x, :, k, 0, :] = c
            fwd[0, x, :, k, 1, :] = -s
            fwd[1, x, :, k, 0, :] = s
            fwd[1, x, :, k, 1, :] = c
            bwd[k, 0, :, 0, x, :] = c
            bwd[k, 0, :, 1, x, :] = s
            bwd[k, 1, :, 0, x, :] = -s
            bwd[k, 1, :, 1, x, :] = c
    left = []
    for m in (fwd.reshape(64, 64), bwd.reshape(64, 64)):
        hi, lo = split_np(m)
        left.append(np.concatenate([hi, lo, hi], axis=1))
    left = np.stack(left)
    lane = np.arange(128)
    j, y = lane // 32, lane % 32
    angle = 2 * np.pi * (np.outer(j, j) / 4 + np.outer(y, y) / 32)
    c, s = np.cos(angle), np.sin(angle)
    right = []
    for m in (np.block([[c, s], [-s, c]]), np.block([[c, -s], [s, c]])):
        right.extend(split_np(m))
    right = np.stack(right)
    row = np.arange(32) // 4
    tw = 2 * np.pi * np.outer(row, j) / 32
    twiddle = np.stack([np.cos(tw), np.sin(tw)]).astype(np.float32)
    return left, right, twiddle


def split(x):
    hi = x.astype(BF16)
    lo = (x - hi.astype(F32)).astype(BF16)
    return hi, lo


def mm(a, b):
    return jnp.dot(a, b, preferred_element_type=F32)


def left_product(table, x):
    hi, lo = split(x)
    return mm(table, jnp.concatenate([hi, hi, lo], axis=0))


def right_product(hi_table, lo_table, x):
    rows = x.shape[0]
    hi, lo = split(x)
    both = mm(jnp.concatenate([hi, lo], axis=0), hi_table)
    return both[:rows] + both[rows:] + mm(hi, lo_table)


def order(i):
    half = (i + 1) // 2
    return 4 + half - 2 * half * (i % 2)


def kernel(
    onsite_hbm, table_hbm, begin_hbm, green_hbm, less_hbm, ret_hbm, adv_hbm, les_hbm,
    left_hbm, right_hbm, twiddle_hbm,
    next_row, derivative,
    onsite, table, begin, green, less, ret, left, right, twiddle,
    raw, slab, oslab, isend, irecv, bsend, brecv, screens, ssend, srecv, sig,
    own, ysend, yrecv, zsend, zrecv, msend, mrecv, orecv, macc, gbuf, hg, first,
    in_sem, os_sem, or_sem, is_sem, ir_sem, gs_sem, gr_sem, ss_sem, sr_sem,
    ys_sem, yr_sem, zs_sem, zr_sem, ms_sem, mr_sem, oq_sem, ready,
):
    ta, ka = lax.axis_index("ta"), lax.axis_index("ka")
    z, y, core = ta // 4, (ta // 2) % 2, ta % 2
    sibling = ta + 1 - 2 * core
    across = ta + 2 - 4 * y
    x, half = ka % 4, ka // 4

    def peer_of(n, sign=1):
        to_half, to_x = PEERS[n]
        return (half + to_half) % 2 * 4 + (x + 4 + sign * to_x) % 4


    loads = [
        pltpu.make_async_copy(src, dst, in_sem.at[i])
        for i, (src, dst) in enumerate(
            (
                (less_hbm, less), (ret_hbm, ret), (green_hbm, green), (table_hbm, table),
                (adv_hbm, raw.at[0]), (les_hbm, raw.at[1]), (onsite_hbm, onsite),
                (begin_hbm, begin), (left_hbm, left), (right_hbm, right), (twiddle_hbm, twiddle),
            )
        )
    ]
    for copy in loads:
        copy.start()

    barrier = pltpu.get_barrier_semaphore()
    for i in range(1, 8):
        pl.semaphore_signal(barrier, inc=1, device_id=(ta, (ka + i) % 8), device_id_type=MESH)
        pl.semaphore_signal(barrier, inc=1, device_id=(sibling, (ka + i) % 8), device_id_type=MESH)
        pl.semaphore_signal(barrier, inc=1, device_id=((ta + 4 * i) % 32, ka), device_id_type=MESH)
    pl.semaphore_signal(barrier, inc=1, device_id=(sibling, ka), device_id_type=MESH)
    pl.semaphore_signal(barrier, inc=1, device_id=(across, ka), device_id_type=MESH)

    for copy in loads[:4]:
        copy.wait()
    for n, ref in enumerate((less, ret, green)):
        for d in range(8):
            isend[d, 8 * n : 8 * n + 8, :] = ref[pl.ds(d, 8, stride=8), :]
    pl.semaphore_wait(barrier, 23)

    def describe(src, dst, ssem, rsem, to):
        return pltpu.make_async_remote_copy(
            src_ref=src, dst_ref=dst, send_sem=ssem, recv_sem=rsem,
            device_id=to, device_id_type=MESH,
        )

    def push(src, dst, ssem, rsem, to):
        describe(src, dst, ssem, rsem, to).start()

    def arrived(dst, rsem):
        describe(dst, dst, rsem, rsem, (sibling, ka)).wait_recv()

    def sent(src, ssem):
        describe(src, src, ssem, ssem, (sibling, ka)).wait_send()

    def exchange(src, dst, ssem, rsem):
        for n in range(7):
            peer = peer_of(n)
            push(src.at[peer], dst.at[ka], ssem.at[n], rsem.at[ka], (ta, peer))
        dst[ka] = src[ka]

    def collect(dst, rsem):
        for i in range(1, 8):
            peer = (ka + i) % 8
            arrived(dst.at[peer], rsem.at[peer])

    exchange(isend, irecv, is_sem, ir_sem)
    for i in range(1, 8):
        pl.semaphore_signal(ready, inc=1, device_id=((ta + 4 * i) % 32, ka), device_id_type=MESH)

    row = lax.broadcasted_iota(jnp.int32, (256, 1), 0)
    col = lax.broadcasted_iota(jnp.int32, (256, 256), 1)
    place = row // 8
    source = (
        ((row // 2) % 4) * 64 + (place % 8) * 8 + ((place // 8) % 2) * 4
        + ((core + place // 16) % 2) * 2 + row % 2
    )
    picked = source == col
    lane = lax.broadcasted_iota(jnp.int32, (1, 256), 1) % 64
    tau = jnp.zeros((1, 256), jnp.int32)
    for i in range(32):
        tau = jnp.where(lane // 2 == i, 2 * table[i], tau)
    tau = tau + lane % 2
    now = 2 * table[ta]
    plain = jnp.where(picked, 1.0, 0.0).astype(BF16)
    masked = [
        jnp.where(picked & (now + s <= tau), 1.0, 0.0).astype(BF16) for s in range(2)
    ]
    for copy in loads[4:]:
        copy.wait()

    def relay(b, carry):
        for kind in range(2):
            for s in range(2):
                parts = [
                    jnp.concatenate([raw[kind, q, b, c, s] for c in range(4)], axis=0)
                    for q in range(2)
                ]
                moved = mm(masked[s] if kind == 0 else plain, jnp.concatenate(parts, axis=1))
                re, im = moved[:, :128], moved[:, 128:]
                d = b * 2 + s
                slab[kind, 0, core * 8 + d] = re[:128].reshape(16, 8, 128)
                slab[kind, 1, core * 8 + d] = im[:128].reshape(16, 8, 128)
                slab[kind, 2, core * 8 + d] = (re[:128] + im[:128]).reshape(16, 8, 128)
                oslab[kind, 0, d] = re[128:].reshape(16, 8, 128)
                oslab[kind, 1, d] = im[128:].reshape(16, 8, 128)
        return carry

    lax.fori_loop(0, 4, relay, 0)
    for kind in range(2):
        for q in range(2):
            push(
                oslab.at[kind, q], slab.at[kind, q, pl.ds(core * 8, 8)],
                os_sem.at[kind, q], or_sem.at[kind, q], (sibling, ka),
            )

    shift = drive_amp * jnp.sin(
        jnp.full((64, 128), drive_freq, F32) * (begin[0] + 64).astype(F32)
    )
    k_lane = lax.broadcasted_iota(jnp.int32, (64, 128), 1)
    k_row = lax.broadcasted_iota(jnp.int32, (64, 128), 0)
    factor = 2.0 * math.pi / KS

    def dispersed(group, lane, by):
        return -2.0 * (
            jnp.cos((4 * group + lane // KS).astype(F32) * factor + by)
            + jnp.cos((lane % KS).astype(F32) * factor)
        )

    e_all = dispersed(k_row // 8, k_lane, shift)
    e = dispersed(ka, k_lane[:8], shift[:8])

    at_row = lax.broadcasted_iota(jnp.int32, (64, 64), 0)
    at_col = lax.broadcasted_iota(jnp.int32, (64, 64), 1)
    entry = jnp.where(at_row // 8 == at_col // 8, at_row % 8 * 8 + at_col % 8, -1)
    turn = jnp.zeros((64, 64), F32)
    for a in range(4):
        for b in range(4):
            o_re, o_im = onsite[0, a, b], onsite[1, a, b]
            turn = jnp.where(entry == 8 * a + b, o_re, turn)
            turn = jnp.where(entry == 8 * (a + 4) + b + 4, o_re, turn)
            turn = jnp.where(entry == 8 * a + b + 4, -o_im, turn)
            turn = jnp.where(entry == 8 * (a + 4) + b, o_im, turn)
    turn_hi, turn_lo = split(turn)
    turn = jnp.concatenate([turn_hi, turn_lo, turn_hi], axis=1)

    tw_c, tw_s = twiddle[0], twiddle[1]

    def to_space(tiles):
        mixed = left_product(left[0], tiles)
        n = tiles.shape[1] // 128
        turned = []
        for i in range(n):
            re, im = (mixed[32 * p : 32 * p + 32, 128 * i : 128 * i + 128] for p in range(2))
            turned.append(
                jnp.concatenate([re * tw_c - im * tw_s, re * tw_s + im * tw_c], axis=1)
            )
        out = right_product(right[0], right[1], jnp.concatenate(turned, axis=0))
        return [out[32 * i : 32 * i + 32] for i in range(n)]

    def to_momenta(fields):
        out = right_product(right[2], right[3], jnp.concatenate(fields, axis=0))
        turned = []
        for i in range(2):
            re, im = out[32 * i : 32 * i + 32, :128], out[32 * i : 32 * i + 32, 128:]
            turned.append(
                jnp.concatenate([re * tw_c + im * tw_s, im * tw_c - re * tw_s], axis=0)
            )
        return left_product(left[1], jnp.concatenate(turned, axis=1))

    collect(irecv, ir_sem)
    tiles = jnp.concatenate(
        [irecv[:, 8 * n : 8 * n + 8, :].reshape(64, 128) for n in range(3)], axis=1
    )
    w_less, w_ret, space = to_space(tiles)
    screens[0] = w_less
    screens[1] = w_ret

    def blocks(js):
        def terms(u, acc):
            kind, half = u // 2, u % 2
            acc = list(acc)
            for v in range(8):
                sd = half * 8 + v
                for q in range(3):
                    values = [slab[kind, q, sd, j] for j in js]
                    for a in range(4):
                        factor = sig[kind, q, sd, a]
                        for n in range(2):
                            at = (n * 4 + a) * 3 + q
                            acc[at] = acc[at] + factor * values[n]
            return tuple(acc)

        zero = jnp.zeros((8, 128), F32)
        flat = lax.fori_loop(0, 4, terms, (zero,) * 24)
        acc = [[flat[(n * 4 + a) * 3 : (n * 4 + a) * 3 + 3] for a in range(4)] for n in range(2)]
        out = []
        for n in range(2):
            re = [acc[n][a][0] - acc[n][a][1] for a in range(4)]
            im = [acc[n][a][2] - acc[n][a][0] - acc[n][a][1] for a in range(4)]
            out.append(re + im)
        return out

    def reduced(r):
        def to_across(piece, carry):
            places = [(z + order(2 * piece + n)) % 8 for n in range(2)]
            out = blocks([(1 - y) * 8 + p for p in places])
            for n in range(2):
                i = 2 * piece + n
                for m in range(8):
                    ysend[r, i, 8 * m : 8 * m + 8] = out[n][m]
                push(ysend.at[r, i], yrecv.at[r, i], ys_sem.at[r, i], yr_sem.at[r, i], (across, ka))
            return carry

        lax.fori_loop(0, 4, to_across, 0)

        def mine(piece, carry):
            places = [(z + order(2 * piece + n)) % 8 for n in range(2)]
            out = blocks([y * 8 + p for p in places])
            for n in range(2):
                for m in range(8):
                    own[2 * piece + n, 8 * m : 8 * m + 8] = out[n][m]
            return carry

        lax.fori_loop(0, 4, mine, 0)

    def to_owner():
        for i in range(8):
            arrived(yrecv.at[2, i], yr_sem.at[2, i])
            if i < 7:
                zsend[i] = own[i] + yrecv[2, i]
                away = (z + order(i)) % 8
                push(
                    zsend.at[i], zrecv.at[z], zs_sem.at[i], zr_sem.at[z],
                    (away * 4 + ta % 4, ka),
                )
        total = own[7] + yrecv[2, 7] + hg[...]
        for i in range(7):
            peer = (z + order(i)) % 8
            arrived(zrecv.at[peer], zr_sem.at[peer])
            total = total + zrecv[peer]
        return total

    def to_fields(r):
        def tiles_of(i):
            arrived(yrecv.at[r, i], yr_sem.at[r, i])
            zsend[i] = own[i] + yrecv[r, i]
            for d in range(8):
                msend[r, i, d] = zsend[i, pl.ds(d, 8, stride=8), :]

        def away_block(i, carry):
            tiles_of(i)
            away = ((z + order(i)) % 8) * 4 + ta % 4
            for n in range(8):
                peer = peer_of(n)
                push(
                    msend.at[r, i, peer], mrecv.at[r, z * 8 + ka], ms_sem.at[r, i],
                    mr_sem.at[r, z], (away, peer),
                )
            return carry

        lax.fori_loop(0, 7, away_block, 0)
        tiles_of(7)
        for n in range(7):
            peer = peer_of(n)
            push(
                msend.at[r, 7, peer], orecv.at[r, n], ms_sem.at[r, 7], oq_sem.at[r], (ta, peer)
            )
        total = hg[...]
        for i in range(7):
            group = pl.ds(((z + order(i)) % 8) * 8, 8)
            arrived(mrecv.at[r, group], mr_sem.at[r, (z + order(i)) % 8])
            total = total + mrecv[r, group].reshape(64, 128)
        macc[...] = total.reshape(8, 8, 128)
        macc[ka] += msend[r, 7, ka]
        arrived(orecv.at[r], oq_sem.at[r])
        for n in range(7):
            macc[peer_of(n, -1)] += orecv[r, n]
        total = macc[...]
        return jnp.concatenate([total[:, 4:], -total[:, :4]], axis=1).reshape(64, 128)

    green_all = irecv[:, 16:24, :].reshape(64, 128)
    state = green_all
    for r in range(3):
        if r > 0:
            (space,) = to_space(state)
        re, im = space[:, :128], space[:, 128:]
        fields = []
        for kind in range(2):
            w_re, w_im = screens[kind, :, :128], screens[kind, :, 128:]
            fields.append(
                jnp.concatenate([-(re * w_im + im * w_re), re * w_re - im * w_im], axis=1)
            )
        sigma = to_momenta(fields)
        for kind in range(2):
            ssend[r, :, kind] = sigma[:, 128 * kind : 128 * kind + 128].reshape(8, 8, 128)
        slot = core * 8 + ka
        for i in range(7):
            peer = peer_of(i)
            for n, to in enumerate((sibling, ta)):
                push(
                    ssend.at[r, peer], srecv.at[r, slot], ss_sem.at[r, 2 * i + n],
                    sr_sem.at[r, slot], (to, peer),
                )
        push(
            ssend.at[r, ka], srecv.at[r, slot], ss_sem.at[r, 14], sr_sem.at[r, slot], (sibling, ka)
        )
        srecv[r, slot] = ssend[r, ka]

        if r < 2:
            hg[...] = left_product(turn, state) + e_all * state
        else:
            for d in range(8):
                bsend[d, :8] = state[8 * d : 8 * d + 8]
                bsend[d, 8:] = first[8 * d : 8 * d + 8]
            exchange(bsend, brecv, gs_sem, gr_sem)

        if r == 0:
            for kind in range(2):
                for q in range(2):
                    theirs = slab.at[kind, q, pl.ds((1 - core) * 8, 8)]
                    arrived(theirs, or_sem.at[kind, q])
                for d in range(8):
                    sd = (1 - core) * 8 + d
                    slab[kind, 2, sd] = slab[kind, 0, sd] + slab[kind, 1, sd]

        for i in range(8):
            peer = (ka + i) % 8
            for n in range(2):
                if i + n > 0:
                    sd = ((core + n) % 2) * 8 + peer
                    arrived(srecv.at[r, sd], sr_sem.at[r, sd])
        for sd in range(16):
            for kind in range(2):
                tile = srecv[r, sd, kind].astype(BF16).astype(F32)
                for a in range(4):
                    s_re = jnp.broadcast_to(tile[a : a + 1], (8, 128))
                    s_im = jnp.broadcast_to(tile[4 + a : 5 + a], (8, 128))
                    sig[kind, 0, sd, a] = s_re
                    sig[kind, 1, sd, a] = s_im
                    sig[kind, 2, sd, a] = s_re + s_im

        if r == 0:
            pl.semaphore_wait(ready, 7)
        reduced(r)
        if r < 2:
            rate = to_fields(r)
            if r == 0:
                first[...] = rate
                state = green_all + time_step * rate
            else:
                state = green_all + (0.5 * time_step) * (first[...] + rate)
            continue

        collect(brecv, gr_sem)
        for d in range(8):
            gbuf[pl.ds(d, 8, stride=8), :] = brecv[d, :8]
            first[pl.ds(d, 8, stride=8), :] = brecv[d, 8:]
        rows = [gbuf[8 * m : 8 * m + 8] for m in range(8)]
        for a in range(4):
            re, im = e * rows[a], e * rows[4 + a]
            for b in range(4):
                o_re, o_im = onsite[0, a, b], onsite[1, a, b]
                re = re + o_re * rows[b] - o_im * rows[4 + b]
                im = im + o_re * rows[4 + b] + o_im * rows[b]
            hg[8 * a : 8 * a + 8] = re
            hg[32 + 8 * a : 40 + 8 * a] = im
        total = to_owner()
        rate = jnp.concatenate([total[32:], -total[:32]], axis=0)
        next_row[...] = green[...] + (0.5 * time_step) * (first[...] + rate)
        derivative[...] = rate

    for kind in range(2):
        for q in range(2):
            sent(oslab.at[kind, q], os_sem.at[kind, q])
    for n in range(7):
        sent(isend.at[peer_of(n)], is_sem.at[n])
        sent(bsend.at[peer_of(n)], gs_sem.at[n])
        sent(zsend.at[n], zs_sem.at[n])
    for r in range(3):
        for i in range(7):
            for n in range(2):
                sent(ssend.at[r, peer_of(i)], ss_sem.at[r, 2 * i + n])
        sent(ssend.at[r, ka], ss_sem.at[r, 14])
        for i in range(8):
            sent(ysend.at[r, i], ys_sem.at[r, i])
        if r < 2:
            for i in range(7):
                sent(msend.at[r, i], ms_sem.at[r, i])
            sent(msend.at[r, 7, pl.ds(0, 7)], ms_sem.at[r, 7])


def local(
    green_row, screen_lesser, screen_retarded, onsite, lesser_slab, advanced_slab, slab_start,
    block_table,
):
    left, right, twiddle = tables()

    def hbm():
        return pl.BlockSpec(memory_space=pltpu.HBM)

    def vmem():
        return pl.BlockSpec(memory_space=pltpu.VMEM)

    def scratch(*dims, kind=F32):
        return pltpu.VMEM(dims, kind)

    def sems(*dims):
        return pltpu.SemaphoreType.DMA(dims)

    rows = jax.ShapeDtypeStruct((64, 128), F32)
    next_row, derivative = pl.pallas_call(
        kernel,
        name="gw_step",
        out_shape=(pltpu.VMEM((64, 128), F32), pltpu.VMEM((64, 128), F32)),
        in_specs=[hbm()] * 11,
        out_specs=(vmem(), vmem()),
        scratch_shapes=[
            pltpu.SMEM((2, 4, 4), F32),
            pltpu.SMEM((32,), jnp.int32),
            pltpu.SMEM((1,), jnp.int32),
            scratch(64, 128),
            scratch(64, 128),
            scratch(64, 128),
            scratch(2, 64, 192, kind=BF16),
            scratch(4, 256, 256, kind=BF16),
            scratch(2, 32, 128),
            scratch(2, 2, 4, 4, 2, 64, 128, kind=BF16),
            scratch(2, 3, 16, 16, 8, 128),
            scratch(2, 2, 8, 16, 8, 128),
            scratch(8, 24, 128),
            scratch(8, 24, 128),
            scratch(8, 16, 128),
            scratch(8, 16, 128),
            scratch(2, 32, 256),
            scratch(3, 8, 2, 8, 128),
            scratch(3, 16, 2, 8, 128),
            scratch(2, 3, 16, 4, 8, 128),
            scratch(8, 64, 128),
            scratch(3, 8, 64, 128),
            scratch(3, 8, 64, 128),
            scratch(8, 64, 128),
            scratch(8, 64, 128),
            scratch(2, 8, 8, 8, 128),
            scratch(2, 64, 8, 128),
            scratch(2, 7, 8, 128),
            scratch(8, 8, 128),
            scratch(64, 128),
            scratch(64, 128),
            scratch(64, 128),
            sems(11),
            sems(2, 2), sems(2, 2),
            sems(8), sems(8),
            sems(8), sems(8),
            sems(3, 16), sems(3, 16),
            sems(3, 8), sems(3, 8),
            sems(7), sems(8),
            sems(2, 8), sems(2, 8), sems(2),
            pltpu.SemaphoreType.REGULAR,
        ],
        compiler_params=pltpu.CompilerParams(
            collective_id=0, has_side_effects=True, vmem_limit_bytes=56 * 2**20
        ),
    )(
        onsite,
        block_table,
        slab_start,
        green_row.reshape(64, 128),
        screen_lesser.reshape(64, 128),
        screen_retarded.reshape(64, 128),
        advanced_slab,
        lesser_slab,
        jnp.asarray(left),
        jnp.asarray(right),
        jnp.asarray(twiddle),
    )
    return next_row.reshape(green_row.shape), derivative.reshape(green_row.shape)


def solution(mesh):
    return jax.shard_map(
        local,
        mesh=mesh,
        in_specs=(
            P(None, None, None, "ta", "ka"),
            P(None, None, None, "ta", "ka"),
            P(None, None, None, "ta", "ka"),
            P(),
            P(None, None, None, "ta", None, "ka"),
            P(None, None, None, "ta", None, "ka"),
            P(),
            P(),
        ),
        out_specs=(P(None, None, None, "ta", "ka"), P(None, None, None, "ta", "ka")),
        check_vma=False,
    )
```

```python
import math

import jax
import jax.numpy as jnp
import numpy as np
from jax import lax
from jax.experimental import pallas as pl
from jax.experimental.pallas import tpu as pltpu
from jax.sharding import PartitionSpec as P

KS = 32
PEERS = ((1, 2), (1, 1), (1, 3), (1, 0), (0, 2), (0, 1), (0, 3), (0, 0))
MESH = pl.DeviceIdType.MESH
F32 = jnp.float32
BF16 = jnp.bfloat16

time_step = 0.1
drive_amp = 1.0
drive_freq = 0.37


def split_np(x):
    hi = x.astype(np.float32).astype(jnp.bfloat16)
    lo = (x - hi.astype(np.float64)).astype(np.float32).astype(jnp.bfloat16)
    return hi, lo


def tables():
    ka, x1 = np.meshgrid(np.arange(8), np.arange(8), indexing="ij")
    c8, s8 = np.cos(2 * np.pi * ka * x1 / 8), np.sin(2 * np.pi * ka * x1 / 8)
    eye = np.eye(4)
    fwd = np.zeros((2, 8, 4, 8, 2, 4))
    bwd = np.zeros((8, 2, 4, 2, 8, 4))
    for k in range(8):
        for x in range(8):
            c, s = c8[k, x] * eye / KS, s8[k, x] * eye / KS
            fwd[0, x, :, k, 0, :] = c
            fwd[0, x, :, k, 1, :] = -s
            fwd[1, x, :, k, 0, :] = s
            fwd[1, x, :, k, 1, :] = c
            bwd[k, 0, :, 0, x, :] = c
            bwd[k, 0, :, 1, x, :] = s
            bwd[k, 1, :, 0, x, :] = -s
            bwd[k, 1, :, 1, x, :] = c
    left = []
    for m in (fwd.reshape(64, 64), bwd.reshape(64, 64)):
        hi, lo = split_np(m)
        left.append(np.concatenate([hi, lo, hi], axis=1))
    left = np.stack(left)
    lane = np.arange(128)
    j, y = lane // 32, lane % 32
    angle = 2 * np.pi * (np.outer(j, j) / 4 + np.outer(y, y) / 32)
    c, s = np.cos(angle), np.sin(angle)
    right = []
    for m in (np.block([[c, s], [-s, c]]), np.block([[c, -s], [s, c]])):
        right.extend(split_np(m))
    right = np.stack(right)
    row = np.arange(32) // 4
    tw = 2 * np.pi * np.outer(row, j) / 32
    twiddle = np.stack([np.cos(tw), np.sin(tw)]).astype(np.float32)
    return left, right, twiddle


def split(x):
    hi = x.astype(BF16)
    lo = (x - hi.astype(F32)).astype(BF16)
    return hi, lo


def mm(a, b):
    return jnp.dot(a, b, preferred_element_type=F32)


def left_product(table, x):
    hi, lo = split(x)
    return mm(table, jnp.concatenate([hi, hi, lo], axis=0))


def right_product(hi_table, lo_table, x):
    rows = x.shape[0]
    hi, lo = split(x)
    both = mm(jnp.concatenate([hi, lo], axis=0), hi_table)
    return both[:rows] + both[rows:] + mm(hi, lo_table)


def order(i):
    half = (i + 1) // 2
    return 4 + half - 2 * half * (i % 2)


def kernel(
    onsite_hbm, table_hbm, begin_hbm, green_hbm, less_hbm, ret_hbm, adv_hbm, les_hbm,
    left_hbm, right_hbm, twiddle_hbm,
    next_row, derivative,
    onsite, table, begin, green, less, ret, left, right, twiddle,
    raw, slab, oslab, isend, irecv, bsend, brecv, screens, ssend, srecv, sig,
    own, ysend, yrecv, zsend, zrecv, msend, mrecv, orecv, macc, gbuf, hg, first,
    in_sem, os_sem, or_sem, is_sem, ir_sem, gs_sem, gr_sem, ss_sem, sr_sem,
    ys_sem, yr_sem, zs_sem, zr_sem, ms_sem, mr_sem, oq_sem, ready,
):
    ta, ka = lax.axis_index("ta"), lax.axis_index("ka")
    z, y, core = ta // 4, (ta // 2) % 2, ta % 2
    sibling = ta + 1 - 2 * core
    across = ta + 2 - 4 * y
    x, half = ka % 4, ka // 4

    def peer_of(n, sign=1):
        to_half, to_x = PEERS[n]
        return (half + to_half) % 2 * 4 + (x + 4 + sign * to_x) % 4


    barrier = pltpu.get_barrier_semaphore()
    for n in range(7):
        for to in (
            (ta, peer_of(n)), (sibling, peer_of(n)), ((z + order(n)) % 8 * 4 + ta % 4, ka)
        ):
            pl.semaphore_signal(barrier, inc=1, device_id=to, device_id_type=MESH)
    pl.semaphore_signal(barrier, inc=1, device_id=(across, ka), device_id_type=MESH)
    pl.semaphore_signal(barrier, inc=1, device_id=(sibling, ka), device_id_type=MESH)

    loads = [
        pltpu.make_async_copy(src, dst, in_sem.at[i])
        for i, (src, dst) in enumerate(
            (
                (less_hbm, less), (ret_hbm, ret), (green_hbm, green), (table_hbm, table),
                (adv_hbm, raw.at[0]), (les_hbm, raw.at[1]), (onsite_hbm, onsite),
                (begin_hbm, begin), (left_hbm, left), (right_hbm, right), (twiddle_hbm, twiddle),
            )
        )
    ]
    for copy in loads:
        copy.start()

    for copy in loads[:4]:
        copy.wait()
    for n, ref in enumerate((less, ret, green)):
        for d in range(8):
            isend[d, 8 * n : 8 * n + 8, :] = ref[pl.ds(d, 8, stride=8), :]
    pl.semaphore_wait(barrier, 23)

    def describe(src, dst, ssem, rsem, to):
        return pltpu.make_async_remote_copy(
            src_ref=src, dst_ref=dst, send_sem=ssem, recv_sem=rsem,
            device_id=to, device_id_type=MESH,
        )

    def push(src, dst, ssem, rsem, to):
        describe(src, dst, ssem, rsem, to).start()

    def arrived(dst, rsem):
        describe(dst, dst, rsem, rsem, (sibling, ka)).wait_recv()

    def sent(src, ssem):
        describe(src, src, ssem, ssem, (sibling, ka)).wait_send()

    def exchange(src, dst, ssem, rsem):
        for n in range(7):
            peer = peer_of(n)
            push(src.at[peer], dst.at[ka], ssem.at[n], rsem.at[ka], (ta, peer))
        dst[ka] = src[ka]

    def collect(dst, rsem):
        for i in range(1, 8):
            peer = (ka + i) % 8
            arrived(dst.at[peer], rsem.at[peer])

    exchange(isend, irecv, is_sem, ir_sem)
    for i in range(1, 8):
        pl.semaphore_signal(ready, inc=1, device_id=((ta + 4 * i) % 32, ka), device_id_type=MESH)

    row = lax.broadcasted_iota(jnp.int32, (256, 1), 0)
    col = lax.broadcasted_iota(jnp.int32, (256, 256), 1)
    place = row // 8
    source = (
        ((row // 2) % 4) * 64 + (place % 8) * 8 + ((place // 8) % 2) * 4
        + ((core + place // 16) % 2) * 2 + row % 2
    )
    picked = source == col
    lane = lax.broadcasted_iota(jnp.int32, (1, 256), 1) % 64
    tau = jnp.zeros((1, 256), jnp.int32)
    for i in range(32):
        tau = jnp.where(lane // 2 == i, 2 * table[i], tau)
    tau = tau + lane % 2
    now = 2 * table[ta]
    plain = jnp.where(picked, 1.0, 0.0).astype(BF16)
    masked = [
        jnp.where(picked & (now + s <= tau), 1.0, 0.0).astype(BF16) for s in range(2)
    ]
    for copy in loads[4:]:
        copy.wait()

    def relay(b, carry):
        for kind in range(2):
            for s in range(2):
                parts = [
                    jnp.concatenate([raw[kind, q, b, c, s] for c in range(4)], axis=0)
                    for q in range(2)
                ]
                moved = mm(masked[s] if kind == 0 else plain, jnp.concatenate(parts, axis=1))
                re, im = moved[:, :128], moved[:, 128:]
                d = b * 2 + s
                slab[kind, 0, core * 8 + d] = re[:128].reshape(16, 8, 128)
                slab[kind, 1, core * 8 + d] = im[:128].reshape(16, 8, 128)
                slab[kind, 2, core * 8 + d] = (re[:128] + im[:128]).reshape(16, 8, 128)
                oslab[kind, 0, d] = re[128:].reshape(16, 8, 128)
                oslab[kind, 1, d] = im[128:].reshape(16, 8, 128)
        return carry

    lax.fori_loop(0, 4, relay, 0)
    for kind in range(2):
        for q in range(2):
            push(
                oslab.at[kind, q], slab.at[kind, q, pl.ds(core * 8, 8)],
                os_sem.at[kind, q], or_sem.at[kind, q], (sibling, ka),
            )

    shift = drive_amp * jnp.sin(
        jnp.full((64, 128), drive_freq, F32) * (begin[0] + 64).astype(F32)
    )
    k_lane = lax.broadcasted_iota(jnp.int32, (64, 128), 1)
    k_row = lax.broadcasted_iota(jnp.int32, (64, 128), 0)
    factor = 2.0 * math.pi / KS

    def dispersed(group, lane, by):
        return -2.0 * (
            jnp.cos((4 * group + lane // KS).astype(F32) * factor + by)
            + jnp.cos((lane % KS).astype(F32) * factor)
        )

    e_all = dispersed(k_row // 8, k_lane, shift)
    e = dispersed(ka, k_lane[:8], shift[:8])

    at_row = lax.broadcasted_iota(jnp.int32, (64, 64), 0)
    at_col = lax.broadcasted_iota(jnp.int32, (64, 64), 1)
    entry = jnp.where(at_row // 8 == at_col // 8, at_row % 8 * 8 + at_col % 8, -1)
    turn = jnp.zeros((64, 64), F32)
    for a in range(4):
        for b in range(4):
            o_re, o_im = onsite[0, a, b], onsite[1, a, b]
            turn = jnp.where(entry == 8 * a + b, o_re, turn)
            turn = jnp.where(entry == 8 * (a + 4) + b + 4, o_re, turn)
            turn = jnp.where(entry == 8 * a + b + 4, -o_im, turn)
            turn = jnp.where(entry == 8 * (a + 4) + b, o_im, turn)
    turn_hi, turn_lo = split(turn)
    turn = jnp.concatenate([turn_hi, turn_lo, turn_hi], axis=1)

    tw_c, tw_s = twiddle[0], twiddle[1]

    def to_space(tiles):
        mixed = left_product(left[0], tiles)
        n = tiles.shape[1] // 128
        turned = []
        for i in range(n):
            re, im = (mixed[32 * p : 32 * p + 32, 128 * i : 128 * i + 128] for p in range(2))
            turned.append(
                jnp.concatenate([re * tw_c - im * tw_s, re * tw_s + im * tw_c], axis=1)
            )
        out = right_product(right[0], right[1], jnp.concatenate(turned, axis=0))
        return [out[32 * i : 32 * i + 32] for i in range(n)]

    def to_momenta(fields):
        out = right_product(right[2], right[3], jnp.concatenate(fields, axis=0))
        turned = []
        for i in range(2):
            re, im = out[32 * i : 32 * i + 32, :128], out[32 * i : 32 * i + 32, 128:]
            turned.append(
                jnp.concatenate([re * tw_c + im * tw_s, im * tw_c - re * tw_s], axis=0)
            )
        return left_product(left[1], jnp.concatenate(turned, axis=1))

    collect(irecv, ir_sem)
    tiles = jnp.concatenate(
        [irecv[:, 8 * n : 8 * n + 8, :].reshape(64, 128) for n in range(3)], axis=1
    )
    w_less, w_ret, space = to_space(tiles)
    screens[0] = w_less
    screens[1] = w_ret

    def blocks(js):
        def terms(u, acc):
            kind, half = u // 2, u % 2
            acc = list(acc)
            for v in range(8):
                sd = half * 8 + v
                for q in range(3):
                    values = [slab[kind, q, sd, j] for j in js]
                    for a in range(4):
                        factor = sig[kind, q, sd, a]
                        for n in range(2):
                            at = (n * 4 + a) * 3 + q
                            acc[at] = acc[at] + factor * values[n]
            return tuple(acc)

        zero = jnp.zeros((8, 128), F32)
        flat = lax.fori_loop(0, 4, terms, (zero,) * 24)
        acc = [[flat[(n * 4 + a) * 3 : (n * 4 + a) * 3 + 3] for a in range(4)] for n in range(2)]
        out = []
        for n in range(2):
            re = [acc[n][a][0] - acc[n][a][1] for a in range(4)]
            im = [acc[n][a][2] - acc[n][a][0] - acc[n][a][1] for a in range(4)]
            out.append(re + im)
        return out

    def reduced(r):
        def to_across(piece, carry):
            places = [(z + order(2 * piece + n)) % 8 for n in range(2)]
            out = blocks([(1 - y) * 8 + p for p in places])
            for n in range(2):
                i = 2 * piece + n
                for m in range(8):
                    ysend[r, i, 8 * m : 8 * m + 8] = out[n][m]
                push(ysend.at[r, i], yrecv.at[r, i], ys_sem.at[r, i], yr_sem.at[r, i], (across, ka))
            return carry

        lax.fori_loop(0, 4, to_across, 0)

        def mine(piece, carry):
            places = [(z + order(2 * piece + n)) % 8 for n in range(2)]
            out = blocks([y * 8 + p for p in places])
            for n in range(2):
                for m in range(8):
                    own[2 * piece + n, 8 * m : 8 * m + 8] = out[n][m]
            return carry

        lax.fori_loop(0, 4, mine, 0)

    def to_owner():
        for i in range(8):
            arrived(yrecv.at[2, i], yr_sem.at[2, i])
            if i < 7:
                zsend[i] = own[i] + yrecv[2, i]
                away = (z + order(i)) % 8
                push(
                    zsend.at[i], zrecv.at[z], zs_sem.at[i], zr_sem.at[z],
                    (away * 4 + ta % 4, ka),
                )
        collect(brecv, gr_sem)
        for d in range(8):
            gbuf[pl.ds(d, 8, stride=8), :] = brecv[d, :8]
            first[pl.ds(d, 8, stride=8), :] = brecv[d, 8:]
        rows = [gbuf[8 * m : 8 * m + 8] for m in range(8)]
        for a in range(4):
            re, im = e * rows[a], e * rows[4 + a]
            for b in range(4):
                o_re, o_im = onsite[0, a, b], onsite[1, a, b]
                re = re + o_re * rows[b] - o_im * rows[4 + b]
                im = im + o_re * rows[4 + b] + o_im * rows[b]
            hg[8 * a : 8 * a + 8] = re
            hg[32 + 8 * a : 40 + 8 * a] = im
        total = own[7] + yrecv[2, 7] + hg[...]
        for i in range(7):
            peer = (z + order(i)) % 8
            arrived(zrecv.at[peer], zr_sem.at[peer])
            total = total + zrecv[peer]
        return total

    def to_fields(r):
        def tiles_of(i):
            arrived(yrecv.at[r, i], yr_sem.at[r, i])
            zsend[i] = own[i] + yrecv[r, i]
            for d in range(8):
                msend[r, i, d] = zsend[i, pl.ds(d, 8, stride=8), :]

        def away_block(i, carry):
            tiles_of(i)
            away = ((z + order(i)) % 8) * 4 + ta % 4
            for n in range(8):
                peer = peer_of(n)
                push(
                    msend.at[r, i, peer], mrecv.at[r, z * 8 + ka], ms_sem.at[r, i],
                    mr_sem.at[r, z], (away, peer),
                )
            return carry

        lax.fori_loop(0, 7, away_block, 0)
        tiles_of(7)
        for n in range(7):
            peer = peer_of(n)
            push(
                msend.at[r, 7, peer], orecv.at[r, n], ms_sem.at[r, 7], oq_sem.at[r], (ta, peer)
            )
        total = hg[...]
        for i in range(7):
            group = pl.ds(((z + order(i)) % 8) * 8, 8)
            arrived(mrecv.at[r, group], mr_sem.at[r, (z + order(i)) % 8])
            total = total + mrecv[r, group].reshape(64, 128)
        macc[...] = total.reshape(8, 8, 128)
        macc[ka] += msend[r, 7, ka]
        arrived(orecv.at[r], oq_sem.at[r])
        for n in range(7):
            macc[peer_of(n, -1)] += orecv[r, n]
        total = macc[...]
        return jnp.concatenate([total[:, 4:], -total[:, :4]], axis=1).reshape(64, 128)

    green_all = irecv[:, 16:24, :].reshape(64, 128)
    state = green_all
    for r in range(3):
        if r > 0:
            (space,) = to_space(state)
        re, im = space[:, :128], space[:, 128:]
        fields = []
        for kind in range(2):
            w_re, w_im = screens[kind, :, :128], screens[kind, :, 128:]
            fields.append(
                jnp.concatenate([-(re * w_im + im * w_re), re * w_re - im * w_im], axis=1)
            )
        sigma = to_momenta(fields)
        for kind in range(2):
            ssend[r, :, kind] = sigma[:, 128 * kind : 128 * kind + 128].reshape(8, 8, 128)
        slot = core * 8 + ka
        for n, to in enumerate((sibling, ta)):
            for i in range(7):
                peer = peer_of(i)
                push(
                    ssend.at[r, peer], srecv.at[r, slot], ss_sem.at[r, 2 * i + n],
                    sr_sem.at[r, slot], (to, peer),
                )
        push(
            ssend.at[r, ka], srecv.at[r, slot], ss_sem.at[r, 14], sr_sem.at[r, slot], (sibling, ka)
        )
        srecv[r, slot] = ssend[r, ka]

        if r < 2:
            hg[...] = left_product(turn, state) + e_all * state
        else:
            for d in range(8):
                bsend[d, :8] = state[8 * d : 8 * d + 8]
                bsend[d, 8:] = first[8 * d : 8 * d + 8]
            exchange(bsend, brecv, gs_sem, gr_sem)

        if r == 0:
            for kind in range(2):
                for q in range(2):
                    theirs = slab.at[kind, q, pl.ds((1 - core) * 8, 8)]
                    arrived(theirs, or_sem.at[kind, q])
                for d in range(8):
                    sd = (1 - core) * 8 + d
                    slab[kind, 2, sd] = slab[kind, 0, sd] + slab[kind, 1, sd]

        for i in range(7, -1, -1):
            for n in range(2):
                sd = ((core + n) % 2) * 8 + peer_of(i)
                if i < 7 or n > 0:
                    arrived(srecv.at[r, sd], sr_sem.at[r, sd])
                for kind in range(2):
                    tile = srecv[r, sd, kind].astype(BF16).astype(F32)
                    for a in range(4):
                        s_re = jnp.broadcast_to(tile[a : a + 1], (8, 128))
                        s_im = jnp.broadcast_to(tile[4 + a : 5 + a], (8, 128))
                        sig[kind, 0, sd, a] = s_re
                        sig[kind, 1, sd, a] = s_im
                        sig[kind, 2, sd, a] = s_re + s_im

        if r == 0:
            pl.semaphore_wait(ready, 7)
        reduced(r)
        if r < 2:
            rate = to_fields(r)
            if r == 0:
                first[...] = rate
                state = green_all + time_step * rate
            else:
                state = green_all + (0.5 * time_step) * (first[...] + rate)
            continue

        total = to_owner()
        rate = jnp.concatenate([total[32:], -total[:32]], axis=0)
        next_row[...] = green[...] + (0.5 * time_step) * (first[...] + rate)
        derivative[...] = rate

    for kind in range(2):
        for q in range(2):
            sent(oslab.at[kind, q], os_sem.at[kind, q])
    for n in range(7):
        sent(isend.at[peer_of(n)], is_sem.at[n])
        sent(bsend.at[peer_of(n)], gs_sem.at[n])
        sent(zsend.at[n], zs_sem.at[n])
    for r in range(3):
        for i in range(7):
            for n in range(2):
                sent(ssend.at[r, peer_of(i)], ss_sem.at[r, 2 * i + n])
        sent(ssend.at[r, ka], ss_sem.at[r, 14])
        for i in range(8):
            sent(ysend.at[r, i], ys_sem.at[r, i])
        if r < 2:
            for i in range(7):
                sent(msend.at[r, i], ms_sem.at[r, i])
            sent(msend.at[r, 7, pl.ds(0, 7)], ms_sem.at[r, 7])


def local(
    green_row, screen_lesser, screen_retarded, onsite, lesser_slab, advanced_slab, slab_start,
    block_table,
):
    left, right, twiddle = tables()

    def hbm():
        return pl.BlockSpec(memory_space=pltpu.HBM)

    def vmem():
        return pl.BlockSpec(memory_space=pltpu.VMEM)

    def scratch(*dims, kind=F32):
        return pltpu.VMEM(dims, kind)

    def sems(*dims):
        return pltpu.SemaphoreType.DMA(dims)

    rows = jax.ShapeDtypeStruct((64, 128), F32)
    next_row, derivative = pl.pallas_call(
        kernel,
        name="gw_step",
        out_shape=(pltpu.VMEM((64, 128), F32), pltpu.VMEM((64, 128), F32)),
        in_specs=[hbm()] * 11,
        out_specs=(vmem(), vmem()),
        scratch_shapes=[
            pltpu.SMEM((2, 4, 4), F32),
            pltpu.SMEM((32,), jnp.int32),
            pltpu.SMEM((1,), jnp.int32),
            scratch(64, 128),
            scratch(64, 128),
            scratch(64, 128),
            scratch(2, 64, 192, kind=BF16),
            scratch(4, 256, 256, kind=BF16),
            scratch(2, 32, 128),
            scratch(2, 2, 4, 4, 2, 64, 128, kind=BF16),
            scratch(2, 3, 16, 16, 8, 128),
            scratch(2, 2, 8, 16, 8, 128),
            scratch(8, 24, 128),
            scratch(8, 24, 128),
            scratch(8, 16, 128),
            scratch(8, 16, 128),
            scratch(2, 32, 256),
            scratch(3, 8, 2, 8, 128),
            scratch(3, 16, 2, 8, 128),
            scratch(2, 3, 16, 4, 8, 128),
            scratch(8, 64, 128),
            scratch(3, 8, 64, 128),
            scratch(3, 8, 64, 128),
            scratch(8, 64, 128),
            scratch(8, 64, 128),
            scratch(2, 8, 8, 8, 128),
            scratch(2, 64, 8, 128),
            scratch(2, 7, 8, 128),
            scratch(8, 8, 128),
            scratch(64, 128),
            scratch(64, 128),
            scratch(64, 128),
            sems(11),
            sems(2, 2), sems(2, 2),
            sems(8), sems(8),
            sems(8), sems(8),
            sems(3, 16), sems(3, 16),
            sems(3, 8), sems(3, 8),
            sems(7), sems(8),
            sems(2, 8), sems(2, 8), sems(2),
            pltpu.SemaphoreType.REGULAR,
        ],
        compiler_params=pltpu.CompilerParams(
            collective_id=0, has_side_effects=True, vmem_limit_bytes=56 * 2**20
        ),
    )(
        onsite,
        block_table,
        slab_start,
        green_row.reshape(64, 128),
        screen_lesser.reshape(64, 128),
        screen_retarded.reshape(64, 128),
        advanced_slab,
        lesser_slab,
        jnp.asarray(left),
        jnp.asarray(right),
        jnp.asarray(twiddle),
    )
    return next_row.reshape(green_row.shape), derivative.reshape(green_row.shape)


def solution(mesh):
    return jax.shard_map(
        local,
        mesh=mesh,
        in_specs=(
            P(None, None, None, "ta", "ka"),
            P(None, None, None, "ta", "ka"),
            P(None, None, None, "ta", "ka"),
            P(),
            P(None, None, None, "ta", None, "ka"),
            P(None, None, None, "ta", None, "ka"),
            P(),
            P(),
        ),
        out_specs=(P(None, None, None, "ta", "ka"), P(None, None, None, "ta", "ka")),
        check_vma=False,
    )
```

```python
import math

import jax
import jax.numpy as jnp
import numpy as np
from jax import lax
from jax.experimental import pallas as pl
from jax.experimental.pallas import tpu as pltpu
from jax.sharding import PartitionSpec as P

KS = 32
PEERS = ((1, 2), (1, 1), (1, 3), (1, 0), (0, 2), (0, 1), (0, 3), (0, 0))
MESH = pl.DeviceIdType.MESH
F32 = jnp.float32
BF16 = jnp.bfloat16

time_step = 0.1
drive_amp = 1.0
drive_freq = 0.37


def split_np(x):
    hi = x.astype(np.float32).astype(jnp.bfloat16)
    lo = (x - hi.astype(np.float64)).astype(np.float32).astype(jnp.bfloat16)
    return hi, lo


def tables():
    ka, x1 = np.meshgrid(np.arange(8), np.arange(8), indexing="ij")
    c8, s8 = np.cos(2 * np.pi * ka * x1 / 8), np.sin(2 * np.pi * ka * x1 / 8)
    eye = np.eye(4)
    fwd = np.zeros((2, 8, 4, 8, 2, 4))
    bwd = np.zeros((8, 2, 4, 2, 8, 4))
    for k in range(8):
        for x in range(8):
            c, s = c8[k, x] * eye / KS, s8[k, x] * eye / KS
            fwd[0, x, :, k, 0, :] = c
            fwd[0, x, :, k, 1, :] = -s
            fwd[1, x, :, k, 0, :] = s
            fwd[1, x, :, k, 1, :] = c
            bwd[k, 0, :, 0, x, :] = c
            bwd[k, 0, :, 1, x, :] = s
            bwd[k, 1, :, 0, x, :] = -s
            bwd[k, 1, :, 1, x, :] = c
    left = []
    for m in (fwd.reshape(64, 64), bwd.reshape(64, 64)):
        hi, lo = split_np(m)
        left.append(np.concatenate([hi, lo, hi], axis=1))
    left = np.stack(left)
    lane = np.arange(128)
    j, y = lane // 32, lane % 32
    angle = 2 * np.pi * (np.outer(j, j) / 4 + np.outer(y, y) / 32)
    c, s = np.cos(angle), np.sin(angle)
    right = []
    for m in (np.block([[c, s], [-s, c]]), np.block([[c, -s], [s, c]])):
        right.extend(split_np(m))
    right = np.stack(right)
    row = np.arange(32) // 4
    tw = 2 * np.pi * np.outer(row, j) / 32
    twiddle = np.stack([np.cos(tw), np.sin(tw)]).astype(np.float32)
    return left, right, twiddle


def split(x):
    hi = x.astype(BF16)
    lo = (x - hi.astype(F32)).astype(BF16)
    return hi, lo


def mm(a, b):
    return jnp.dot(a, b, preferred_element_type=F32)


def left_product(table, x):
    hi, lo = split(x)
    return mm(table, jnp.concatenate([hi, hi, lo], axis=0))


def right_product(hi_table, lo_table, x):
    rows = x.shape[0]
    hi, lo = split(x)
    both = mm(jnp.concatenate([hi, lo], axis=0), hi_table)
    return both[:rows] + both[rows:] + mm(hi, lo_table)


def order(i):
    half = (i + 1) // 2
    return 4 + half - 2 * half * (i % 2)


def kernel(
    onsite_hbm, table_hbm, begin_hbm, green_hbm, less_hbm, ret_hbm, adv_hbm, les_hbm,
    left_hbm, right_hbm, twiddle_hbm,
    next_row, derivative,
    onsite, table, begin, green, less, ret, left, right, twiddle,
    raw, slab, oslab, isend, irecv, bsend, brecv, screens, ssend, srecv, sig,
    own, ysend, yrecv, zsend, zrecv, msend, mrecv, orecv, macc, gbuf, hg, first,
    in_sem, os_sem, or_sem, is_sem, ir_sem, gs_sem, gr_sem, ss_sem, sr_sem,
    ys_sem, yr_sem, zs_sem, zr_sem, ms_sem, mr_sem, oq_sem, ready,
):
    ta, ka = lax.axis_index("ta"), lax.axis_index("ka")
    z, y, core = ta // 4, (ta // 2) % 2, ta % 2
    sibling = ta + 1 - 2 * core
    across = ta + 2 - 4 * y
    x, half = ka % 4, ka // 4

    def peer_of(n, sign=1):
        to_half, to_x = PEERS[n]
        return (half + to_half) % 2 * 4 + (x + 4 + sign * to_x) % 4


    barrier = pltpu.get_barrier_semaphore()
    for n in range(7):
        for to in (
            (ta, peer_of(n)), (sibling, peer_of(n)), ((z + order(n)) % 8 * 4 + ta % 4, ka)
        ):
            pl.semaphore_signal(barrier, inc=1, device_id=to, device_id_type=MESH)
    pl.semaphore_signal(barrier, inc=1, device_id=(across, ka), device_id_type=MESH)
    pl.semaphore_signal(barrier, inc=1, device_id=(sibling, ka), device_id_type=MESH)

    loads = [
        pltpu.make_async_copy(src, dst, in_sem.at[i])
        for i, (src, dst) in enumerate(
            (
                (less_hbm, less), (ret_hbm, ret), (green_hbm, green), (table_hbm, table),
                (adv_hbm, raw.at[0]), (les_hbm, raw.at[1]), (onsite_hbm, onsite),
                (begin_hbm, begin), (left_hbm, left), (right_hbm, right), (twiddle_hbm, twiddle),
            )
        )
    ]
    for copy in loads:
        copy.start()

    for copy in loads[:4]:
        copy.wait()
    for n, ref in enumerate((less, ret, green)):
        for d in range(8):
            isend[d, 8 * n : 8 * n + 8, :] = ref[pl.ds(d, 8, stride=8), :]
    pl.semaphore_wait(barrier, 23)

    def describe(src, dst, ssem, rsem, to):
        return pltpu.make_async_remote_copy(
            src_ref=src, dst_ref=dst, send_sem=ssem, recv_sem=rsem,
            device_id=to, device_id_type=MESH,
        )

    def push(src, dst, ssem, rsem, to):
        describe(src, dst, ssem, rsem, to).start()

    def arrived(dst, rsem):
        describe(dst, dst, rsem, rsem, (sibling, ka)).wait_recv()

    def sent(src, ssem):
        describe(src, src, ssem, ssem, (sibling, ka)).wait_send()

    def exchange(src, dst, ssem, rsem):
        for n in range(7):
            peer = peer_of(n)
            push(src.at[peer], dst.at[ka], ssem.at[n], rsem.at[ka], (ta, peer))
        dst[ka] = src[ka]

    def collect(dst, rsem):
        for i in range(1, 8):
            peer = (ka + i) % 8
            arrived(dst.at[peer], rsem.at[peer])

    exchange(isend, irecv, is_sem, ir_sem)
    for i in range(1, 8):
        pl.semaphore_signal(ready, inc=1, device_id=((ta + 4 * i) % 32, ka), device_id_type=MESH)

    row = lax.broadcasted_iota(jnp.int32, (256, 1), 0)
    col = lax.broadcasted_iota(jnp.int32, (256, 256), 1)
    place = row // 8
    source = (
        ((row // 2) % 4) * 64 + (place % 8) * 8 + ((place // 8) % 2) * 4
        + ((core + place // 16) % 2) * 2 + row % 2
    )
    picked = source == col
    lane = lax.broadcasted_iota(jnp.int32, (1, 256), 1) % 64
    tau = jnp.zeros((1, 256), jnp.int32)
    for i in range(32):
        tau = jnp.where(lane // 2 == i, 2 * table[i], tau)
    tau = tau + lane % 2
    now = 2 * table[ta]
    plain = jnp.where(picked, 1.0, 0.0).astype(BF16)
    masked = [
        jnp.where(picked & (now + s <= tau), 1.0, 0.0).astype(BF16) for s in range(2)
    ]
    for copy in loads[4:]:
        copy.wait()

    def relay(b, carry):
        for kind in range(2):
            for s in range(2):
                parts = [
                    jnp.concatenate([raw[kind, q, b, c, s] for c in range(4)], axis=0)
                    for q in range(2)
                ]
                moved = mm(masked[s] if kind == 0 else plain, jnp.concatenate(parts, axis=1))
                re, im = moved[:, :128], moved[:, 128:]
                d = b * 2 + s
                slab[kind, 0, core * 8 + d] = re[:128].reshape(16, 8, 128)
                slab[kind, 1, core * 8 + d] = im[:128].reshape(16, 8, 128)
                slab[kind, 2, core * 8 + d] = (re[:128] + im[:128]).reshape(16, 8, 128)
                oslab[kind, 0, d] = re[128:].reshape(16, 8, 128)
                oslab[kind, 1, d] = im[128:].reshape(16, 8, 128)
        return carry

    lax.fori_loop(0, 4, relay, 0)
    for kind in range(2):
        for q in range(2):
            push(
                oslab.at[kind, q], slab.at[kind, q, pl.ds(core * 8, 8)],
                os_sem.at[kind, q], or_sem.at[kind, q], (sibling, ka),
            )

    shift = drive_amp * jnp.sin(
        jnp.full((64, 128), drive_freq, F32) * (begin[0] + 64).astype(F32)
    )
    k_lane = lax.broadcasted_iota(jnp.int32, (64, 128), 1)
    k_row = lax.broadcasted_iota(jnp.int32, (64, 128), 0)
    factor = 2.0 * math.pi / KS

    def dispersed(group, lane, by):
        return -2.0 * (
            jnp.cos((4 * group + lane // KS).astype(F32) * factor + by)
            + jnp.cos((lane % KS).astype(F32) * factor)
        )

    e_all = dispersed(k_row // 8, k_lane, shift)
    e = dispersed(ka, k_lane[:8], shift[:8])

    at_row = lax.broadcasted_iota(jnp.int32, (64, 64), 0)
    at_col = lax.broadcasted_iota(jnp.int32, (64, 64), 1)
    entry = jnp.where(at_row // 8 == at_col // 8, at_row % 8 * 8 + at_col % 8, -1)
    turn = jnp.zeros((64, 64), F32)
    for a in range(4):
        for b in range(4):
            o_re, o_im = onsite[0, a, b], onsite[1, a, b]
            turn = jnp.where(entry == 8 * a + b, o_re, turn)
            turn = jnp.where(entry == 8 * (a + 4) + b + 4, o_re, turn)
            turn = jnp.where(entry == 8 * a + b + 4, -o_im, turn)
            turn = jnp.where(entry == 8 * (a + 4) + b, o_im, turn)
    turn_hi, turn_lo = split(turn)
    turn = jnp.concatenate([turn_hi, turn_lo, turn_hi], axis=1)

    tw_c, tw_s = twiddle[0], twiddle[1]

    def to_space(tiles):
        mixed = left_product(left[0], tiles)
        n = tiles.shape[1] // 128
        turned = []
        for i in range(n):
            re, im = (mixed[32 * p : 32 * p + 32, 128 * i : 128 * i + 128] for p in range(2))
            turned.append(
                jnp.concatenate([re * tw_c - im * tw_s, re * tw_s + im * tw_c], axis=1)
            )
        out = right_product(right[0], right[1], jnp.concatenate(turned, axis=0))
        return [out[32 * i : 32 * i + 32] for i in range(n)]

    def to_momenta(fields):
        out = right_product(right[2], right[3], jnp.concatenate(fields, axis=0))
        turned = []
        for i in range(2):
            re, im = out[32 * i : 32 * i + 32, :128], out[32 * i : 32 * i + 32, 128:]
            turned.append(
                jnp.concatenate([re * tw_c + im * tw_s, im * tw_c - re * tw_s], axis=0)
            )
        return left_product(left[1], jnp.concatenate(turned, axis=1))

    collect(irecv, ir_sem)
    tiles = jnp.concatenate(
        [irecv[:, 8 * n : 8 * n + 8, :].reshape(64, 128) for n in range(3)], axis=1
    )
    w_less, w_ret, space = to_space(tiles)
    screens[0] = w_less
    screens[1] = w_ret

    def blocks(js):
        def terms(kind, acc):
            acc = list(acc)
            for sd in range(16):
                for q in range(3):
                    values = [slab[kind, q, sd, j] for j in js]
                    for a in range(4):
                        factor = sig[kind, q, sd, a]
                        for n in range(2):
                            at = (n * 4 + a) * 3 + q
                            acc[at] = acc[at] + factor * values[n]
            return tuple(acc)

        zero = jnp.zeros((8, 128), F32)
        flat = lax.fori_loop(0, 2, terms, (zero,) * 24)
        acc = [[flat[(n * 4 + a) * 3 : (n * 4 + a) * 3 + 3] for a in range(4)] for n in range(2)]
        out = []
        for n in range(2):
            re = [acc[n][a][0] - acc[n][a][1] for a in range(4)]
            im = [acc[n][a][2] - acc[n][a][0] - acc[n][a][1] for a in range(4)]
            out.append(re + im)
        return out

    def reduced(r):
        def to_across(piece, carry):
            places = [(z + order(2 * piece + n)) % 8 for n in range(2)]
            out = blocks([(1 - y) * 8 + p for p in places])
            for n in range(2):
                i = 2 * piece + n
                for m in range(8):
                    ysend[r, i, 8 * m : 8 * m + 8] = out[n][m]
                for part in range(2):
                    rows = pl.ds(32 * part, 32)
                    push(
                        ysend.at[r, i, rows], yrecv.at[r, i, rows], ys_sem.at[r, i],
                        yr_sem.at[r, i], (across, ka),
                    )
            return carry

        lax.fori_loop(0, 4, to_across, 0)

        def mine(piece, carry):
            places = [(z + order(2 * piece + n)) % 8 for n in range(2)]
            out = blocks([y * 8 + p for p in places])
            for n in range(2):
                for m in range(8):
                    own[2 * piece + n, 8 * m : 8 * m + 8] = out[n][m]
            return carry

        lax.fori_loop(0, 4, mine, 0)

    def to_owner():
        for i in range(8):
            arrived(yrecv.at[2, i], yr_sem.at[2, i])
            if i < 7:
                zsend[i] = own[i] + yrecv[2, i]
                away = (z + order(i)) % 8
                push(
                    zsend.at[i], zrecv.at[z], zs_sem.at[i], zr_sem.at[z],
                    (away * 4 + ta % 4, ka),
                )
        collect(brecv, gr_sem)
        for d in range(8):
            gbuf[pl.ds(d, 8, stride=8), :] = brecv[d, :8]
            first[pl.ds(d, 8, stride=8), :] = brecv[d, 8:]
        rows = [gbuf[8 * m : 8 * m + 8] for m in range(8)]
        for a in range(4):
            re, im = e * rows[a], e * rows[4 + a]
            for b in range(4):
                o_re, o_im = onsite[0, a, b], onsite[1, a, b]
                re = re + o_re * rows[b] - o_im * rows[4 + b]
                im = im + o_re * rows[4 + b] + o_im * rows[b]
            hg[8 * a : 8 * a + 8] = re
            hg[32 + 8 * a : 40 + 8 * a] = im
        total = own[7] + yrecv[2, 7] + hg[...]
        for i in range(7):
            peer = (z + order(i)) % 8
            arrived(zrecv.at[peer], zr_sem.at[peer])
            total = total + zrecv[peer]
        return total

    def to_fields(r):
        def tiles_of(i):
            arrived(yrecv.at[r, i], yr_sem.at[r, i])
            zsend[i] = own[i] + yrecv[r, i]
            for d in range(8):
                msend[r, i, d] = zsend[i, pl.ds(d, 8, stride=8), :]

        def away_block(i, carry):
            tiles_of(i)
            away = ((z + order(i)) % 8) * 4 + ta % 4
            for n in range(8):
                peer = peer_of(n)
                push(
                    msend.at[r, i, peer], mrecv.at[r, z * 8 + ka], ms_sem.at[r, i],
                    mr_sem.at[r, z], (away, peer),
                )
            return carry

        lax.fori_loop(0, 7, away_block, 0)
        tiles_of(7)
        for n in range(7):
            peer = peer_of(n)
            push(
                msend.at[r, 7, peer], orecv.at[r, n], ms_sem.at[r, 7], oq_sem.at[r], (ta, peer)
            )
        total = hg[...]
        for i in range(7):
            group = pl.ds(((z + order(i)) % 8) * 8, 8)
            arrived(mrecv.at[r, group], mr_sem.at[r, (z + order(i)) % 8])
            total = total + mrecv[r, group].reshape(64, 128)
        macc[...] = total.reshape(8, 8, 128)
        macc[ka] += msend[r, 7, ka]
        arrived(orecv.at[r], oq_sem.at[r])
        for n in range(7):
            macc[peer_of(n, -1)] += orecv[r, n]
        total = macc[...]
        return jnp.concatenate([total[:, 4:], -total[:, :4]], axis=1).reshape(64, 128)

    green_all = irecv[:, 16:24, :].reshape(64, 128)
    state = green_all
    for r in range(3):
        if r > 0:
            (space,) = to_space(state)
        re, im = space[:, :128], space[:, 128:]
        fields = []
        for kind in range(2):
            w_re, w_im = screens[kind, :, :128], screens[kind, :, 128:]
            fields.append(
                jnp.concatenate([-(re * w_im + im * w_re), re * w_re - im * w_im], axis=1)
            )
        sigma = to_momenta(fields)
        for kind in range(2):
            ssend[r, :, kind] = sigma[:, 128 * kind : 128 * kind + 128].reshape(8, 8, 128)
        slot = core * 8 + ka
        for n, to in enumerate((sibling, ta)):
            for i in range(7):
                peer = peer_of(i)
                push(
                    ssend.at[r, peer], srecv.at[r, slot], ss_sem.at[r, 2 * i + n],
                    sr_sem.at[r, slot], (to, peer),
                )
        push(
            ssend.at[r, ka], srecv.at[r, slot], ss_sem.at[r, 14], sr_sem.at[r, slot], (sibling, ka)
        )
        srecv[r, slot] = ssend[r, ka]

        if r < 2:
            hg[...] = left_product(turn, state) + e_all * state
        else:
            for d in range(8):
                bsend[d, :8] = state[8 * d : 8 * d + 8]
                bsend[d, 8:] = first[8 * d : 8 * d + 8]
            exchange(bsend, brecv, gs_sem, gr_sem)

        if r == 0:
            for kind in range(2):
                for q in range(2):
                    theirs = slab.at[kind, q, pl.ds((1 - core) * 8, 8)]
                    arrived(theirs, or_sem.at[kind, q])
                for d in range(8):
                    sd = (1 - core) * 8 + d
                    slab[kind, 2, sd] = slab[kind, 0, sd] + slab[kind, 1, sd]

        for i in range(7, -1, -1):
            for n in range(2):
                sd = ((core + n) % 2) * 8 + peer_of(i)
                if i < 7 or n > 0:
                    arrived(srecv.at[r, sd], sr_sem.at[r, sd])
                for kind in range(2):
                    tile = srecv[r, sd, kind].astype(BF16).astype(F32)
                    for a in range(4):
                        s_re = jnp.broadcast_to(tile[a : a + 1], (8, 128))
                        s_im = jnp.broadcast_to(tile[4 + a : 5 + a], (8, 128))
                        sig[kind, 0, sd, a] = s_re
                        sig[kind, 1, sd, a] = s_im
                        sig[kind, 2, sd, a] = s_re + s_im

        if r == 0:
            pl.semaphore_wait(ready, 7)
        reduced(r)
        if r < 2:
            rate = to_fields(r)
            if r == 0:
                first[...] = rate
                state = green_all + time_step * rate
            else:
                state = green_all + (0.5 * time_step) * (first[...] + rate)
            continue

        total = to_owner()
        rate = jnp.concatenate([total[32:], -total[:32]], axis=0)
        next_row[...] = green[...] + (0.5 * time_step) * (first[...] + rate)
        derivative[...] = rate

    for kind in range(2):
        for q in range(2):
            sent(oslab.at[kind, q], os_sem.at[kind, q])
    for n in range(7):
        sent(isend.at[peer_of(n)], is_sem.at[n])
        sent(bsend.at[peer_of(n)], gs_sem.at[n])
        sent(zsend.at[n], zs_sem.at[n])
    for r in range(3):
        for i in range(7):
            for n in range(2):
                sent(ssend.at[r, peer_of(i)], ss_sem.at[r, 2 * i + n])
        sent(ssend.at[r, ka], ss_sem.at[r, 14])
        for i in range(8):
            sent(ysend.at[r, i], ys_sem.at[r, i])
        if r < 2:
            for i in range(7):
                sent(msend.at[r, i], ms_sem.at[r, i])
            sent(msend.at[r, 7, pl.ds(0, 7)], ms_sem.at[r, 7])


def local(
    green_row, screen_lesser, screen_retarded, onsite, lesser_slab, advanced_slab, slab_start,
    block_table,
):
    left, right, twiddle = tables()

    def hbm():
        return pl.BlockSpec(memory_space=pltpu.HBM)

    def vmem():
        return pl.BlockSpec(memory_space=pltpu.VMEM)

    def scratch(*dims, kind=F32):
        return pltpu.VMEM(dims, kind)

    def sems(*dims):
        return pltpu.SemaphoreType.DMA(dims)

    rows = jax.ShapeDtypeStruct((64, 128), F32)
    next_row, derivative = pl.pallas_call(
        kernel,
        name="gw_step",
        out_shape=(pltpu.VMEM((64, 128), F32), pltpu.VMEM((64, 128), F32)),
        in_specs=[hbm()] * 11,
        out_specs=(vmem(), vmem()),
        scratch_shapes=[
            pltpu.SMEM((2, 4, 4), F32),
            pltpu.SMEM((32,), jnp.int32),
            pltpu.SMEM((1,), jnp.int32),
            scratch(64, 128),
            scratch(64, 128),
            scratch(64, 128),
            scratch(2, 64, 192, kind=BF16),
            scratch(4, 256, 256, kind=BF16),
            scratch(2, 32, 128),
            scratch(2, 2, 4, 4, 2, 64, 128, kind=BF16),
            scratch(2, 3, 16, 16, 8, 128),
            scratch(2, 2, 8, 16, 8, 128),
            scratch(8, 24, 128),
            scratch(8, 24, 128),
            scratch(8, 16, 128),
            scratch(8, 16, 128),
            scratch(2, 32, 256),
            scratch(3, 8, 2, 8, 128),
            scratch(3, 16, 2, 8, 128),
            scratch(2, 3, 16, 4, 8, 128),
            scratch(8, 64, 128),
            scratch(3, 8, 64, 128),
            scratch(3, 8, 64, 128),
            scratch(8, 64, 128),
            scratch(8, 64, 128),
            scratch(2, 8, 8, 8, 128),
            scratch(2, 64, 8, 128),
            scratch(2, 7, 8, 128),
            scratch(8, 8, 128),
            scratch(64, 128),
            scratch(64, 128),
            scratch(64, 128),
            sems(11),
            sems(2, 2), sems(2, 2),
            sems(8), sems(8),
            sems(8), sems(8),
            sems(3, 16), sems(3, 16),
            sems(3, 8), sems(3, 8),
            sems(7), sems(8),
            sems(2, 8), sems(2, 8), sems(2),
            pltpu.SemaphoreType.REGULAR,
        ],
        compiler_params=pltpu.CompilerParams(
            collective_id=0, has_side_effects=True, vmem_limit_bytes=56 * 2**20
        ),
    )(
        onsite,
        block_table,
        slab_start,
        green_row.reshape(64, 128),
        screen_lesser.reshape(64, 128),
        screen_retarded.reshape(64, 128),
        advanced_slab,
        lesser_slab,
        jnp.asarray(left),
        jnp.asarray(right),
        jnp.asarray(twiddle),
    )
    return next_row.reshape(green_row.shape), derivative.reshape(green_row.shape)


def solution(mesh):
    return jax.shard_map(
        local,
        mesh=mesh,
        in_specs=(
            P(None, None, None, "ta", "ka"),
            P(None, None, None, "ta", "ka"),
            P(None, None, None, "ta", "ka"),
            P(),
            P(None, None, None, "ta", None, "ka"),
            P(None, None, None, "ta", None, "ka"),
            P(),
            P(),
        ),
        out_specs=(P(None, None, None, "ta", "ka"), P(None, None, None, "ta", "ka")),
        check_vma=False,
    )
```
